32 devices in a mesh: fsdp: 8 (over y, x, core), tp: 4 (over z).
Axes of the slice: x: 2, y: 2, z: 4, core: 2. Of those that a mesh axis runs over, the one named last changes fastest.
Arguments:
- inputs: bfloat16 [16384, 1024], P(('fsdp', 'tp')), may hold values from -6 to 6
- seq_lengths: int32 [8, 7], P('fsdp'), may hold values from 1 to 512, 2048 in all within a row
- qkv_w: bfloat16 [3, 1024, 1024], P(None, 'fsdp', 'tp'), may hold values from -0.1875 to 0.1875
- out_w: bfloat16 [1024, 1024], P('tp', 'fsdp'), may hold values from -1 to 1
- fc_w: bfloat16 [1024, 4096], P('fsdp', 'tp'), may hold values from -0.1875 to 0.1875
- proj_w: bfloat16 [4096, 1024], P('tp', 'fsdp'), may hold values from -0.125 to 0.125
- ln1_gain: bfloat16 [1024], P(('fsdp', 'tp')), may hold values from 0.099609375 to 1.8984375
- ln1_bias: bfloat16 [1024], P(('fsdp', 'tp')), may hold values from -1.1953125 to 1.1953125
- q_bias: bfloat16 [1024], P(('fsdp', 'tp')), may hold values from -3 to 3
- v_bias: bfloat16 [1024], P(('fsdp', 'tp')), may hold values from -0.29882812 to 0.29882812
- out_bias: bfloat16 [1024], P(('fsdp', 'tp')), may hold values from -1.796875 to 1.796875
- ln2_gain: bfloat16 [1024], P(('fsdp', 'tp')), may hold values from 0.099609375 to 1.8984375
- ln2_bias: bfloat16 [1024], P(('fsdp', 'tp')), may hold values from -1.1953125 to 1.1953125
- fc_bias: bfloat16 [4096], P(('fsdp', 'tp')), may hold values from -1.796875 to 1.796875
- proj_bias: bfloat16 [1024], P(('fsdp', 'tp')), may hold values from -1.796875 to 1.796875
- cotangent: bfloat16 [16384, 1024], P(('fsdp', 'tp')), may hold values from -6 to 6
Outputs:
- outputs: float32 [16384, 1024], P(('fsdp', 'tp'))
- dinputs: float32 [16384, 1024], P(('fsdp', 'tp'))
- dqkv_w: float32 [3, 1024, 1024], P(None, 'fsdp', 'tp')
- dout_w: float32 [1024, 1024], P('tp', 'fsdp')
- dfc_w: float32 [1024, 4096], P('fsdp', 'tp')
- dproj_w: float32 [4096, 1024], P('tp', 'fsdp')
- dln1_gain: float32 [1024], P(('fsdp', 'tp'))
- dln1_bias: float32 [1024], P(('fsdp', 'tp'))
- dq_bias: float32 [1024], P(('fsdp', 'tp'))
- dv_bias: float32 [1024], P(('fsdp', 'tp'))
- dout_bias: float32 [1024], P(('fsdp', 'tp'))
- dln2_gain: float32 [1024], P(('fsdp', 'tp'))
- dln2_bias: float32 [1024], P(('fsdp', 'tp'))
- dfc_bias: float32 [4096], P(('fsdp', 'tp'))
- dproj_bias: float32 [1024], P(('fsdp', 'tp'))
The draws below stay inside these ranges and needn't reach their ends.
Inputs may be any that keep to these rules, and one draw needn't show every extreme that they name: `seq_lengths`: each row lists the lengths of the 7 sequences packed in order into the 2048 tokens of one packed row; they sum to 2048 and the longest is exactly 512.
All inputs are finite; a program needn't handle non-finite values.
Results may differ from the reference program's by a relative error of at most 0.014.
Values may be sent and summed in bfloat16 or wider, within the bound.
No kernel may reach another device: no remote copies, remote signals or barrier semaphores. Data moves between devices by JAX's collectives and lax.ppermute only.
A program may use at most 192 MiB of HBM per device.

```python
import math
from functools import partial
import jax
import jax.numpy as jnp
import numpy as np
from jax import lax

D = 1024
HEADS = 16
HD = 64
FF = 4096
SEQ_MAX = 512
ROW = 2048
SEQS = 7
TOKENS = 16384
N_FSDP = 8


def strengthened(result, stream_key, source, target, parts, factor):
    owner, partner = [(jnp.arange(result.shape[position]) // (result.shape[position] // parts)).reshape([-1 if axis == position else 1 for axis in range(result.ndim)]) for position in (source, target)]
    chosen = jax.random.permutation(stream_key, parts)[partner]
    strong = (owner == chosen) | (owner == (partner + parts // 2) % parts)
    return jnp.where(strong, factor * result, result)


def level_of(rng, shape, shards, least, top_value):
    def one(dim, shards_of):
        steps = jax.random.uniform(jax.random.fold_in(jax.random.fold_in(rng, 6), dim), (shards_of,), jnp.float32, least / len(shards), top_value / len(shards))
        return jnp.repeat(jnp.exp(steps), shape[dim] // shards_of).reshape((-1,) + (1,) * (len(shape) - dim - 1))

    factor_of = one(*shards[0])
    for cut in shards[1:]:
        factor_of = factor_of * one(*cut)
    return factor_of


def profile(count, total, reach, skew):
    loads = [(1 << 20) // math.isqrt(rank ** skew) + 1 for rank in range(2, count + 1)]
    spare, given = total - reach - (count - 1), [1] * (count - 1)
    while spare > 0:
        candidates = [i for i in range(count - 1) if given[i] < reach]
        pool, left = sum([loads[i] for i in candidates]), spare
        for i in candidates:
            extra = min(reach - given[i], max(1, left * loads[i] // pool), spare)
            given[i] = given[i] + extra
            spare = spare - extra
    return np.array([reach] + given)


def ragged_sizes(own_key, number_of, total, most, lean):
    if number_of == 2:
        one = jax.random.randint(own_key, (), max(1, total - most), min(most, total - 1) + 1)
        return jnp.stack([one, total - one])
    sizes = jnp.asarray(profile(number_of, total, most, lean), jnp.int32)
    twos = (number_of - 1) // 2
    donor, taker = sizes[1:1 + 2 * twos:2], sizes[2:2 + 2 * twos:2]
    margin = jnp.minimum(donor - 1, most - taker)
    passed = jax.random.randint(jax.random.fold_in(own_key, 1), (twos,), 0, 1 << 20) % (margin + 1)
    sizes = sizes.at[1:1 + 2 * twos:2].set(donor - passed).at[2:2 + 2 * twos:2].set(taker + passed)
    return sizes[jax.random.permutation(jax.random.fold_in(own_key, 2), number_of)]


def gaussian(own_key, dims, scale, bound, pieces=(), kind=jnp.bfloat16):
    values = jax.random.normal(own_key, dims, jnp.float32) * scale
    if len(pieces) > 0:
        values = level_of(own_key, dims, pieces, -0.22, 0.18) * values
    return jnp.clip(values, min=-bound, max=bound).astype(kind)


def heavy_noise(rng, extent, deviation, most, shards, heavy, kind=jnp.bfloat16):
    drawn = deviation * jax.random.normal(rng, extent, jnp.float32)
    if shards:
        drawn = drawn * level_of(rng, extent, shards, -0.22, 0.18)
    return jnp.clip(strengthened(drawn, jax.random.fold_in(rng, 3), *heavy), -most, most).astype(kind)


def setup_inputs(seed: int = 0) -> dict:
    seeds = jax.random.split(jax.random.key(seed), 17)
    return {
        "inputs": gaussian(seeds[0], (TOKENS, D), 1.0, 6.0, ((0, 32),)),
        "seq_lengths": jax.vmap(lambda own: ragged_sizes(own, SEQS, ROW, SEQ_MAX, 2))(jax.random.split(seeds[1], N_FSDP)).reshape((N_FSDP, SEQS)).astype(jnp.int32),
        "qkv_w": gaussian(seeds[2], (3, D, D), D ** -0.5, 0.1875, ((1, 8), (2, 4))),
        "out_w": gaussian(seeds[3], (D, D), (D // 32) ** -0.5, 1.0, ((0, 4), (1, 8))),
        "fc_w": gaussian(seeds[4], (D, FF), D ** -0.5, 0.1875, ((0, 8), (1, 4))),
        "proj_w": gaussian(seeds[5], (FF, D), (FF // 2) ** -0.5, 0.125, ((0, 4), (1, 8))),
        "ln1_gain": jnp.clip(1.0 + 0.18 * jax.random.normal(seeds[6], (D,), jnp.float32), 0.099609375, 1.8984375).astype(jnp.bfloat16),
        "ln1_bias": gaussian(seeds[7], (D,), 0.2, 1.1953125, ((0, 32),)),
        "q_bias": gaussian(seeds[8], (D,), 0.5, 3.0, ((0, 32),)),
        "v_bias": gaussian(seeds[9], (D,), 0.05, 0.29882812, ((0, 32),)),
        "out_bias": gaussian(seeds[10], (D,), 0.3, 1.796875, ((0, 32),)),
        "ln2_gain": jnp.clip(1.0 + 0.18 * jax.random.normal(seeds[11], (D,), jnp.float32), 0.099609375, 1.8984375).astype(jnp.bfloat16),
        "ln2_bias": gaussian(seeds[12], (D,), 0.2, 1.1953125, ((0, 32),)),
        "fc_bias": gaussian(seeds[13], (FF,), 0.3, 1.796875, ((0, 32),)),
        "proj_bias": gaussian(seeds[14], (D,), 0.3, 1.796875, ((0, 32),)),
        "cotangent": heavy_noise(seeds[15], (TOKENS, D), 1.0, 6.0, ((0, 32),), (0, 1, 32, 2.75)),
    }


@jax.custom_vjp
def low(v):
    return lax.optimization_barrier(v.astype(jnp.bfloat16)).astype(jnp.float32)

@jax.custom_vjp
def low_back(v):
    return v

def low_keep(v):
    return (low(v), None)

def low_pass(kept, grad):
    return (grad,)

def back_keep(v):
    return (v, None)

def back_low(kept, grad):
    return (low(grad),)
low.defvjp(low_keep, low_pass)
low_back.defvjp(back_keep, back_low)
HIGHEST = lax.Precision.HIGHEST
EPSILON = 1e-05
MASKED = -1e+30

def layer_norm(values, gain, shift):
    center = lax.optimization_barrier(jnp.mean(values, axis=-1, keepdims=True))
    offset = values - center
    spread = lax.optimization_barrier(jnp.mean(offset * offset, axis=-1, keepdims=True))
    return offset * lax.rsqrt(spread + EPSILON) * gain + shift

def segment_of(lengths, count):
    ends = jnp.cumsum(lengths.astype(jnp.int32))
    places = jnp.arange(count, dtype=jnp.int32)
    return lax.optimization_barrier(jnp.sum((places[:, None] >= ends[None, :]).astype(jnp.int32), axis=1))

def softmax_rows(scores):
    peak = lax.optimization_barrier(jnp.max(scores, axis=-1, keepdims=True))
    expo = jnp.exp(scores - peak)
    return expo / lax.optimization_barrier(jnp.sum(expo, axis=-1, keepdims=True))

def row_forward(row, segment, params):
    qkv_w, out_w, fc_w, proj_w, ln1_gain, ln1_bias, q_bias, v_bias, out_bias, ln2_gain, ln2_bias, fc_bias, proj_bias = params
    count = row.shape[0]
    first = low(layer_norm(row, ln1_gain, ln1_bias))
    queries = low(low_back(jnp.dot(first, qkv_w[0], precision=HIGHEST) + q_bias))
    key_rows = low(low_back(jnp.dot(first, qkv_w[1], precision=HIGHEST)))
    values = low(low_back(jnp.dot(first, qkv_w[2], precision=HIGHEST) + v_bias))
    places = jnp.arange(count, dtype=jnp.int32)
    allowed = (places[None, :] <= places[:, None]) & (segment[None, :] == segment[:, None])
    scale = HD ** (-0.5)

    def by_head(matrix):
        return matrix.reshape(count, HEADS, HD).transpose(1, 0, 2)

    def one_head(triple):
        head_q, head_k, head_v = triple
        scores = jnp.dot(head_q, head_k.T, precision=HIGHEST) * scale
        scores = low_back(jnp.where(allowed, scores, MASKED))
        attend = low(softmax_rows(scores))
        return jnp.dot(attend, head_v, precision=HIGHEST)
    context = lax.map(jax.checkpoint(one_head), (by_head(queries), by_head(key_rows), by_head(values)))
    context = low(low_back(context.transpose(1, 0, 2).reshape(count, HEADS * HD)))
    attn_out = low_back(jnp.dot(context, out_w, precision=HIGHEST) + out_bias)
    middle = row + attn_out
    second = low(layer_norm(middle, ln2_gain, ln2_bias))
    pre_act = low_back(jnp.dot(second, fc_w, precision=HIGHEST) + fc_bias)
    hidden = low(jax.nn.gelu(pre_act, approximate=True))
    return middle + low_back(jnp.dot(hidden, proj_w, precision=HIGHEST) + proj_bias)

def reference(inputs, seq_lengths, qkv_w, out_w, fc_w, proj_w, ln1_gain, ln1_bias, q_bias, v_bias, out_bias, ln2_gain, ln2_bias, fc_bias, proj_bias, cotangent):
    params = tuple((item.astype(jnp.float32) for item in (qkv_w, out_w, fc_w, proj_w, ln1_gain, ln1_bias, q_bias, v_bias, out_bias, ln2_gain, ln2_bias, fc_bias, proj_bias)))
    rows = inputs.astype(jnp.float32).reshape(N_FSDP, ROW, D)
    segments = jax.vmap(partial(segment_of, count=ROW))(seq_lengths)

    def forward(rows, params):

        def per_row(pair):
            return row_forward(pair[0], pair[1], params)
        return lax.map(jax.checkpoint(per_row), (rows, segments))
    outputs, pullback = jax.vjp(forward, rows, params)
    drows, dparams = pullback(cotangent.astype(jnp.float32).reshape(N_FSDP, ROW, D))
    dqkv_w, dout_w, dfc_w, dproj_w, dln1_gain, dln1_bias, dq_bias, dv_bias, dout_bias, dln2_gain, dln2_bias, dfc_bias, dproj_bias = dparams
    return (outputs.reshape(TOKENS, D), drows.reshape(TOKENS, D), dqkv_w, dout_w, dfc_w, dproj_w, dln1_gain, dln1_bias, dq_bias, dv_bias, dout_bias, dln2_gain, dln2_bias, dfc_bias, dproj_bias)
```

```python
from functools import partial

import jax
import jax.numpy as jnp
from jax import lax
from jax.experimental import pallas as pl
from jax.experimental.pallas import tpu as pltpu
from jax.sharding import PartitionSpec as P

HD = 64
QT = 256
EPSILON = 1e-05
MASKED = -1e30
BF = jnp.bfloat16
F32 = jnp.float32


def layer_norm(values, gain, shift):
    center = jnp.mean(values, axis=-1, keepdims=True)
    offset = values - center
    spread = jnp.mean(offset * offset, axis=-1, keepdims=True)
    return offset * lax.rsqrt(spread + EPSILON) * gain + shift


def gelu(values):
    return jax.nn.gelu(values, approximate=True)


def exchange(item, axis, mask):
    size = lax.axis_size(axis)
    return lax.ppermute(item, axis, [(i, i ^ mask) for i in range(size)])


def exchange_by_core(item, even_mask, odd_mask):
    size = lax.axis_size("fsdp")
    pairs = [(i, i ^ (odd_mask if i % 2 else even_mask)) for i in range(size)]
    return lax.ppermute(item, "fsdp", pairs)


def rotate(item, step):
    size = lax.axis_size("tp")
    return lax.ppermute(item, "tp", [(i, (i + step) % size) for i in range(size)])


def step_masks():
    bits = [1 << b for b in range(1, lax.axis_size("fsdp").bit_length() - 1)]
    return list(zip(bits, bits[::-1]))


def held_offsets():
    held = [(0, 0)]
    for even, odd in step_masks():
        held = held + [(a ^ even, b ^ odd) for a, b in held]
    return held


def absolute(offsets):
    mine = lax.axis_index("fsdp")
    return mine ^ jnp.where(mine % 2 == 0, offsets[0], offsets[1])


def gather_tp(part):
    size = lax.axis_size("tp")
    mine = lax.axis_index("tp")
    got = [part] + [rotate(part, k) for k in range(1, size)]
    return jnp.concatenate(
        [lax.select_n((mine - p) % size, *got) for p in range(size)], axis=-1
    )


def gather_weight(part):
    slab = gather_tp(part)
    held = [(slab, 0, 0)]
    for even, odd in step_masks():
        held = held + [
            (exchange_by_core(item, even, odd), a ^ even, b ^ odd) for item, a, b in held
        ]
    held = held + [(exchange(item, "fsdp", 1), b ^ 1, a ^ 1) for item, a, b in held]
    count = lax.axis_size("fsdp")
    n, rows, cols = slab.shape
    whole = jnp.zeros((n, count, rows, cols), part.dtype)
    for item, a, b in held:
        whole = lax.dynamic_update_slice(
            whole, item[:, None], (0, absolute((a, b)), 0, 0)
        )
    return whole.reshape(n, count * rows, cols)


def scatter_weight(grad):
    count = lax.axis_size("fsdp")
    size = lax.axis_size("tp")
    n, all_rows, all_cols = grad.shape
    rows, cols = all_rows // count, all_cols // size
    blocks = grad.reshape(n, count, rows, all_cols)

    def block(offsets):
        return lax.dynamic_slice(
            blocks, (0, absolute(offsets), 0, 0), (n, 1, rows, all_cols)
        )[:, 0]

    held = {}
    for a, b in held_offsets():
        got = exchange(block((a ^ 1, b ^ 1)), "fsdp", 1)
        held[(a, b)] = got
    mixed = {}
    for a, b in held_offsets():
        mixed[(a, b)] = (block((a, b)).astype(F32) + held[(b, a)].astype(F32)).astype(BF)
    held = mixed
    for even, odd in step_masks()[::-1]:
        keep = list(held)[: len(held) // 2]
        held = {
            (a, b): (
                held[(a, b)].astype(F32)
                + exchange_by_core(held[(a ^ even, b ^ odd)], even, odd).astype(F32)
            ).astype(BF)
            for a, b in keep
        }
    slab = held[(0, 0)]
    mine = lax.axis_index("tp")
    parts = [slab[:, :, p * cols : (p + 1) * cols] for p in range(size)]
    total = lax.select_n(mine, *parts).astype(F32)
    for k in range(1, size):
        total = total + rotate(lax.select_n((mine + k) % size, *parts), k).astype(F32)
    return total


def gather_vectors(vectors):
    pack = jnp.concatenate(vectors)[None, None]
    size = lax.axis_size("tp")
    mine = lax.axis_index("tp")
    got = [pack] + [rotate(pack, k) for k in range(1, size)]
    pack = jnp.concatenate(
        [lax.select_n((mine - p) % size, *got) for p in range(size)], axis=1
    )
    where = lax.axis_index("fsdp")
    for b in range(lax.axis_size("fsdp").bit_length() - 1):
        other = exchange(pack, "fsdp", 1 << b)
        high = (where >> b) % 2 == 1
        pack = jnp.concatenate(
            [jnp.where(high, other, pack), jnp.where(high, pack, other)], axis=0
        )
    out, at = [], 0
    for item in vectors:
        out.append(pack[:, :, at : at + item.shape[0]].reshape(-1).astype(F32))
        at += item.shape[0]
    return out


def scatter_vectors(vectors):
    count = lax.axis_size("fsdp")
    size = lax.axis_size("tp")
    pack = jnp.concatenate([v.reshape(count, size, -1) for v in vectors], axis=2)
    where = lax.axis_index("fsdp")
    for b in range(count.bit_length() - 1)[::-1]:
        half = pack.shape[0] // 2
        high = (where >> b) % 2 == 1
        low_part, high_part = pack[:half], pack[half:]
        keep = jnp.where(high, high_part, low_part)
        send = jnp.where(high, low_part, high_part)
        pack = keep + exchange(send, "fsdp", 1 << b)
    pack = pack[0]
    mine = lax.axis_index("tp")
    rows = [pack[p] for p in range(size)]
    total = lax.select_n(mine, *rows)
    for k in range(1, size):
        total = total + rotate(lax.select_n((mine + k) % size, *rows), k)
    out, at = [], 0
    for v in vectors:
        length = v.shape[0] // (count * size)
        out.append(total[at : at + length])
        at += length
    return out


def head_lanes(shape, head):
    lane = lax.broadcasted_iota(jnp.int32, shape, 1)
    return (lane >= head * HD) & (lane < (head + 1) * HD)


def nt(left, right):
    return lax.dot_general(left, right, (((1,), (1,)), ((), ())), preferred_element_type=F32)


def nn(left, right):
    return lax.dot_general(left, right, (((1,), (0,)), ((), ())), preferred_element_type=F32)


def allowed_keys(lo_row, start, keys, queries, rows):
    key = start + lax.broadcasted_iota(jnp.int32, (keys, queries), 0)
    query = rows + start + lax.broadcasted_iota(jnp.int32, (keys, queries), 1)
    return (key >= lo_row) & (key <= query)


def attend_forward(lo_ref, q_ref, k_ref, v_ref, ctx_ref, lse_ref):
    rows = q_ref.shape[0]
    width = rows + QT
    value_t = v_ref[...].T
    for tile in range(rows // QT):
        start = tile * QT
        query = q_ref[pl.ds(start, QT), :] * jnp.asarray(HD**-0.5, BF)
        keys = k_ref[pl.ds(start, width), :]
        allowed = allowed_keys(lo_ref[:, start : start + QT], start, width, QT, rows)
        parts = []
        for head in range(2):
            query_h = jnp.where(head_lanes(query.shape, head), query, jnp.zeros_like(query))
            scores = jnp.where(allowed, nt(keys, query_h), MASKED)
            peak = jnp.max(scores, axis=0, keepdims=True)
            expo = jnp.exp(scores - peak)
            total = jnp.sum(expo, axis=0, keepdims=True)
            attend = (expo * (1.0 / total)).astype(BF)
            parts.append(
                nn(value_t[head * HD : (head + 1) * HD, start : start + width], attend)
            )
            lse_ref[0, head : head + 1, start : start + QT] = peak + jnp.log(total)
        ctx_ref[pl.ds(start, QT), :] = jnp.concatenate(parts, axis=0).T.astype(BF)


def attend_backward(
    lo_ref, q_ref, k_ref, v_ref, ctx_ref, lse_ref, grad_ref, dq_ref, dk_ref, dv_ref, dk_acc, dv_acc
):
    rows = q_ref.shape[0]
    width = rows + QT
    scale = HD**-0.5
    dk_acc[...] = jnp.zeros_like(dk_acc)
    dv_acc[...] = jnp.zeros_like(dv_acc)
    key_t = k_ref[...].T
    for tile in range(rows // QT):
        start = tile * QT
        query = q_ref[pl.ds(start, QT), :] * jnp.asarray(scale, BF)
        grad = grad_ref[pl.ds(start, QT), :]
        keys = k_ref[pl.ds(start, width), :]
        values = v_ref[pl.ds(start, width), :]
        allowed = allowed_keys(lo_ref[:, start : start + QT], start, width, QT, rows)
        inner_t = (grad.astype(F32) * ctx_ref[pl.ds(start, QT), :].astype(F32)).T
        parts = []
        dk_sum, dv_sum = None, None
        for head in range(2):
            lanes = head_lanes(query.shape, head)
            query_h = jnp.where(lanes, query, jnp.zeros_like(query))
            grad_h = jnp.where(lanes, grad, jnp.zeros_like(grad))
            scores = jnp.where(allowed, nt(keys, query_h), MASKED)
            attend = jnp.exp(scores - lse_ref[0, head : head + 1, start : start + QT])
            inner = jnp.sum(inner_t[head * HD : (head + 1) * HD, :], axis=0, keepdims=True)
            dscores = (attend * (nt(values, grad_h) - inner)).astype(BF)
            dv_part = nn(attend.astype(BF), grad_h)
            dk_part = nn(dscores, query_h)
            dv_sum = dv_part if dv_sum is None else dv_sum + dv_part
            dk_sum = dk_part if dk_sum is None else dk_sum + dk_part
            parts.append(
                nn(key_t[head * HD : (head + 1) * HD, start : start + width], dscores) * scale
            )
        dq_ref[pl.ds(start, QT), :] = jnp.concatenate(parts, axis=0).T.astype(BF)
        dk_acc[pl.ds(start, width), :] += dk_sum
        dv_acc[pl.ds(start, width), :] += dv_sum
    dk_ref[...] = dk_acc[...].astype(BF)
    dv_ref[...] = dv_acc[...].astype(BF)


LANES = 2 * HD


def columns(rows):
    return pl.BlockSpec((rows, LANES), lambda pair: (0, pair))


def attention_forward(lo, queries, key_rows, values):
    rows, width = queries.shape
    pairs = width // LANES
    return pl.pallas_call(
        attend_forward,
        grid=(pairs,),
        in_specs=[
            pl.BlockSpec((1, rows), lambda pair: (0, 0)),
            columns(rows),
            columns(2 * rows),
            columns(2 * rows),
        ],
        out_specs=[columns(rows), pl.BlockSpec((1, 2, rows), lambda pair: (pair, 0, 0))],
        out_shape=[
            jax.ShapeDtypeStruct((rows, width), BF),
            jax.ShapeDtypeStruct((pairs, 2, rows), F32),
        ],
        compiler_params=pltpu.CompilerParams(vmem_limit_bytes=48 * 2**20),
        name="attend_forward",
    )(lo, queries, key_rows, values)


def attention_backward(lo, queries, key_rows, values, context, lse, dcontext):
    rows, width = queries.shape
    pairs = width // LANES
    return pl.pallas_call(
        attend_backward,
        grid=(pairs,),
        in_specs=[
            pl.BlockSpec((1, rows), lambda pair: (0, 0)),
            columns(rows),
            columns(2 * rows),
            columns(2 * rows),
            columns(rows),
            pl.BlockSpec((1, 2, rows), lambda pair: (pair, 0, 0)),
            columns(rows),
        ],
        out_specs=[columns(rows), columns(2 * rows), columns(2 * rows)],
        out_shape=[
            jax.ShapeDtypeStruct((rows, width), BF),
            jax.ShapeDtypeStruct((2 * rows, width), BF),
            jax.ShapeDtypeStruct((2 * rows, width), BF),
        ],
        scratch_shapes=[
            pltpu.VMEM((2 * rows, LANES), F32),
            pltpu.VMEM((2 * rows, LANES), F32),
        ],
        compiler_params=pltpu.CompilerParams(vmem_limit_bytes=48 * 2**20),
        name="attend_backward",
    )(lo, queries, key_rows, values, context, lse, dcontext)


def lowest_keys(lengths, rows):
    count = lengths.shape[0]
    step = jnp.arange(count, dtype=jnp.int32)
    ends = jnp.sum(jnp.where(step[None, :] <= step[:, None], lengths[None, :], 0), axis=1)
    base = lax.axis_index("tp") * rows
    places = base + jnp.arange(rows, dtype=jnp.int32)
    begins = jnp.max(jnp.where(ends[:, None] <= places[None, :], ends[:, None], 0), axis=0)
    return (begins - base + rows).astype(jnp.int32)[None, :]


def per_device(
    inputs,
    seq_lengths,
    qkv_w,
    out_w,
    fc_w,
    proj_w,
    ln1_gain,
    ln1_bias,
    q_bias,
    v_bias,
    out_bias,
    ln2_gain,
    ln2_bias,
    fc_bias,
    proj_bias,
    cotangent,
):
    rows = inputs.shape[0]
    (
        gain_one,
        shift_one,
        query_shift,
        value_shift,
        attn_shift,
        gain_two,
        shift_two,
        hidden_shift,
        mlp_shift,
    ) = gather_vectors(
        [ln1_gain, ln1_bias, q_bias, v_bias, out_bias, ln2_gain, ln2_bias, fc_bias, proj_bias]
    )
    tp_size = lax.axis_size("tp")
    before = lax.ppermute(inputs, "tp", [(i, i + 1) for i in range(tp_size - 1)])
    qkv_full = gather_weight(qkv_w)
    out_full = gather_weight(out_w.T[None])[0]
    fc_full = gather_weight(fc_w[None])[0]
    proj_full = gather_weight(proj_w.T[None])[0]

    lo = lowest_keys(seq_lengths[0], rows)
    residual = inputs.astype(F32)
    first_f, pull_one = jax.vjp(layer_norm, residual, gain_one, shift_one)
    first = first_f.astype(BF)
    first_before = layer_norm(before.astype(F32), gain_one, shift_one).astype(BF)
    first_both = jnp.concatenate([first_before, first], axis=0)
    queries = (
        jnp.dot(first, qkv_full[0], preferred_element_type=F32) + query_shift
    ).astype(BF)
    key_rows = jnp.dot(first_both, qkv_full[1], preferred_element_type=F32).astype(BF)
    values = (
        jnp.dot(first_both, qkv_full[2], preferred_element_type=F32) + value_shift
    ).astype(BF)
    context, lse = attention_forward(lo, queries, key_rows, values)
    attn_out = jnp.einsum("rj,ij->ri", context, out_full, preferred_element_type=F32)
    middle = residual + attn_out + attn_shift
    second_f, pull_two = jax.vjp(layer_norm, middle, gain_two, shift_two)
    second = second_f.astype(BF)
    pre_act = jnp.dot(second, fc_full, preferred_element_type=F32) + hidden_shift
    hidden_f, pull_gelu = jax.vjp(gelu, pre_act)
    hidden = hidden_f.astype(BF)
    dproj_full = jnp.einsum("ri,rj->ij", cotangent, hidden, preferred_element_type=F32)
    dproj_w = scatter_weight(dproj_full.astype(BF)[None])[0].T
    dhidden = jnp.dot(cotangent, proj_full, preferred_element_type=F32)
    dpre = pull_gelu(dhidden)[0].astype(BF)
    dfc_full = jnp.einsum("ri,rj->ij", second, dpre, preferred_element_type=F32)
    dfc_w = scatter_weight(dfc_full.astype(BF)[None])[0]
    dsecond = jnp.einsum("rj,ij->ri", dpre, fc_full, preferred_element_type=F32)
    mlp_out = jnp.einsum("rj,ij->ri", hidden, proj_full, preferred_element_type=F32)
    outputs = middle + mlp_out + mlp_shift

    dmiddle_norm, dgain_two, dshift_two = pull_two(dsecond)
    dmiddle = cotangent.astype(F32) + dmiddle_norm
    dattn = dmiddle.astype(BF)
    dcontext = jnp.dot(dattn, out_full, preferred_element_type=F32).astype(BF)
    dqueries, dkeys, dvalues = attention_backward(
        lo, queries, key_rows, values, context, lse, dcontext
    )
    dqkv_full = jnp.stack(
        [
            jnp.einsum("ri,rj->ij", first, dqueries, preferred_element_type=F32).astype(BF),
            jnp.einsum("ri,rj->ij", first_both, dkeys, preferred_element_type=F32).astype(BF),
            jnp.einsum("ri,rj->ij", first_both, dvalues, preferred_element_type=F32).astype(BF),
        ]
    )
    dqkv_w = scatter_weight(dqkv_full)
    dout_full = jnp.einsum("ri,rj->ij", dattn, context, preferred_element_type=F32)
    dout_w = scatter_weight(dout_full.astype(BF)[None])[0].T

    dfirst_both = jnp.einsum(
        "rj,ij->ri", dkeys, qkv_full[1], preferred_element_type=F32
    ) + jnp.einsum("rj,ij->ri", dvalues, qkv_full[2], preferred_element_type=F32)
    dfirst_after = lax.ppermute(
        dfirst_both[:rows].astype(BF), "tp", [(i + 1, i) for i in range(tp_size - 1)]
    )
    dfirst = (
        dfirst_both[rows:]
        + jnp.einsum("rj,ij->ri", dqueries, qkv_full[0], preferred_element_type=F32)
        + dfirst_after.astype(F32)
    )
    dresidual, dgain_one, dshift_one = pull_one(dfirst)
    dinputs = dmiddle + dresidual
    vector_grads = scatter_vectors(
        [
            dgain_one,
            dshift_one,
            jnp.sum(dqueries, axis=0, dtype=F32),
            jnp.sum(dvalues, axis=0, dtype=F32),
            jnp.sum(dattn, axis=0, dtype=F32),
            dgain_two,
            dshift_two,
            jnp.sum(dpre, axis=0, dtype=F32),
            jnp.sum(cotangent, axis=0, dtype=F32),
        ]
    )
    return (outputs, dinputs, dqkv_w, dout_w, dfc_w, dproj_w, *vector_grads)


def solution(mesh):
    vector = P(("fsdp", "tp"))
    tokens = P(("fsdp", "tp"), None)
    weights = (P(None, "fsdp", "tp"), P("tp", "fsdp"), P("fsdp", "tp"), P("tp", "fsdp"))
    return jax.shard_map(
        per_device,
        mesh=mesh,
        in_specs=(tokens, P("fsdp", None), *weights, *([vector] * 9), tokens),
        out_specs=(tokens, tokens, *weights, *([vector] * 9)),
        check_vma=False,
    )
```

```python
import jax
import jax.numpy as jnp
from jax import lax
import numpy as np
from jax.experimental import pallas as pl
from jax.experimental.pallas import tpu as pltpu
from jax.sharding import PartitionSpec as P

HD = 64
QT = 256
EPSILON = 1e-05
MASKED = -1e30
BF = jnp.bfloat16
F32 = jnp.float32


def layer_norm(values, gain, shift):
    center = jnp.mean(values, axis=-1, keepdims=True)
    offset = values - center
    spread = jnp.mean(offset * offset, axis=-1, keepdims=True)
    return offset * lax.rsqrt(spread + EPSILON) * gain + shift


def gelu(values):
    return jax.nn.gelu(values, approximate=True)


def exchange(item, axis, mask):
    size = lax.axis_size(axis)
    return lax.ppermute(item, axis, [(i, i ^ mask) for i in range(size)])


def exchange_by_core(item, even_mask, odd_mask):
    size = lax.axis_size("fsdp")
    pairs = [(i, i ^ (odd_mask if i % 2 else even_mask)) for i in range(size)]
    return lax.ppermute(item, "fsdp", pairs)


def rotate(item, step):
    size = lax.axis_size("tp")
    return lax.ppermute(item, "tp", [(i, (i + step) % size) for i in range(size)])


def step_masks():
    bits = [1 << b for b in range(1, lax.axis_size("fsdp").bit_length() - 1)]
    return list(zip(bits, bits[::-1]))


def slot_blocks():
    held = [(0, 0)]
    for even, odd in step_masks():
        held = held + [(a ^ even, b ^ odd) for a, b in held]
    held = held + [(b ^ 1, a ^ 1) for a, b in held]
    table = np.asarray(held, np.int32)
    mine = lax.axis_index("fsdp")
    return mine ^ jnp.where(mine % 2 == 0, table[:, 0], table[:, 1])


def gather_tp(part):
    size = lax.axis_size("tp")
    mine = lax.axis_index("tp")
    got = [part] + [rotate(part, k) for k in range(1, size)]
    return jnp.concatenate(
        [lax.select_n((mine - p) % size, *got) for p in range(size)], axis=-1
    )


def gather_step(held, masks):
    for even, odd in masks:
        held = jnp.concatenate([held, exchange_by_core(held, even, odd)], axis=1)
    return held


def add_low(left, right):
    return (left.astype(F32) + right.astype(F32)).astype(BF)


def halves(left, right):
    half = left.shape[1] // 2
    return (
        add_low(left[:, :half], right[:, :half]),
        add_low(left[:, half:], right[:, half:]),
    )


def scatter_core(own, other):
    return halves(own, exchange(other, "fsdp", 1))


def scatter_step(keep, send, masks):
    for even, odd in masks[:-1]:
        keep, send = halves(keep, exchange_by_core(send, even, odd))
    even, odd = masks[-1]
    got = exchange_by_core(send, even, odd)
    return keep, got


def scatter_tp(slab):
    size = lax.axis_size("tp")
    mine = lax.axis_index("tp")
    cols = slab.shape[-1] // size
    parts = [slab[:, :, p * cols : (p + 1) * cols] for p in range(size)]
    total = lax.select_n(mine, *parts).astype(F32)
    for k in range(1, size):
        total = total + rotate(lax.select_n((mine + k) % size, *parts), k).astype(F32)
    return total


def join(*items):
    return lax.optimization_barrier(items)


def pick(items, order):
    slot = jnp.arange(items.shape[0], dtype=jnp.int32)
    chosen = (order[:, None] == slot[None, :]).reshape(
        (items.shape[0],) * 2 + (1,) * (items.ndim - 1)
    )
    return jnp.sum(jnp.where(chosen, items[None], jnp.zeros_like(items)[None]), axis=1).astype(
        items.dtype
    )


def inverse(blocks):
    slot = jnp.arange(blocks.shape[0], dtype=jnp.int32)
    return jnp.sum(jnp.where(blocks[None, :] == slot[:, None], slot[None, :], 0), axis=1)


def reorder(values, blocks, back=False):
    rows, width = values.shape
    count = blocks.shape[0]
    lanes = width // count
    if lanes % 128:
        order = inverse(blocks) if back else blocks
        split = pick(values.reshape(rows, count, lanes).swapaxes(0, 1), order)
        return split.swapaxes(0, 1).reshape(rows, width)

    def body(_, source, target):
        target[...] = source[...]

    plain = pl.BlockSpec((rows, lanes), lambda j, table: (0, j))
    moved = pl.BlockSpec((rows, lanes), lambda j, table: (0, table[j]))
    return pl.pallas_call(
        body,
        grid_spec=pltpu.PrefetchScalarGridSpec(
            num_scalar_prefetch=1,
            grid=(count,),
            in_specs=[plain if back else moved],
            out_specs=moved if back else plain,
        ),
        out_shape=jax.ShapeDtypeStruct(values.shape, values.dtype),
        name="reorder",
    )(blocks, values)


def gather_vectors(vectors, which, blocks):
    pack = jnp.concatenate(vectors)[None, None]
    size = lax.axis_size("tp")
    mine = lax.axis_index("tp")
    got = [pack] + [rotate(pack, k) for k in range(1, size)]
    pack = jnp.concatenate(
        [lax.select_n((mine - p) % size, *got) for p in range(size)], axis=1
    )
    where = lax.axis_index("fsdp")
    for b in range(lax.axis_size("fsdp").bit_length() - 1):
        other = exchange(pack, "fsdp", 1 << b)
        high = (where >> b) % 2 == 1
        pack = jnp.concatenate(
            [jnp.where(high, other, pack), jnp.where(high, pack, other)], axis=0
        )
    moved = pick(pack, blocks)
    out, at = [], 0
    for item, exchanged in zip(vectors, which):
        source = moved if exchanged else pack
        out.append(source[:, :, at : at + item.shape[0]].reshape(1, -1).astype(F32))
        at += item.shape[0]
    return out


def scatter_vectors(vectors, which, blocks):
    count = lax.axis_size("fsdp")
    size = lax.axis_size("tp")
    packs = [
        jnp.concatenate(
            [v.reshape(count, size, -1) for v, m in zip(vectors, which) if m == kind], axis=2
        )
        for kind in (True, False)
    ]
    pack = jnp.concatenate([pick(packs[0], inverse(blocks)), packs[1]], axis=2)
    where = lax.axis_index("fsdp")
    for b in range(count.bit_length() - 1)[::-1]:
        half = pack.shape[0] // 2
        high = (where >> b) % 2 == 1
        low_part, high_part = pack[:half], pack[half:]
        keep = jnp.where(high, high_part, low_part)
        send = jnp.where(high, low_part, high_part)
        pack = keep + exchange(send, "fsdp", 1 << b)
    pack = pack[0]
    mine = lax.axis_index("tp")
    rows = [pack[p] for p in range(size)]
    total = lax.select_n(mine, *rows)
    for k in range(1, size):
        total = total + rotate(lax.select_n((mine + k) % size, *rows), k)
    out, at = {}, 0
    for kind in (True, False):
        for i, v in enumerate(vectors):
            if which[i] == kind:
                length = v.size // (count * size)
                out[i] = total[at : at + length]
                at += length
    return [out[i] for i in range(len(vectors))]


def head_lanes(shape, head):
    lane = lax.broadcasted_iota(jnp.int32, shape, 1)
    return (lane >= head * HD) & (lane < (head + 1) * HD)


def nt(left, right):
    return lax.dot_general(left, right, (((1,), (1,)), ((), ())), preferred_element_type=F32)


def nn(left, right):
    return lax.dot_general(left, right, (((1,), (0,)), ((), ())), preferred_element_type=F32)


def allowed_keys(lo_row, start, keys, queries, rows):
    key = start + lax.broadcasted_iota(jnp.int32, (keys, queries), 0)
    query = rows + start + lax.broadcasted_iota(jnp.int32, (keys, queries), 1)
    return (key >= lo_row) & (key <= query)


def attend_forward(lo_ref, q_ref, k_ref, v_ref, ctx_ref, lse_ref):
    rows = q_ref.shape[0]
    width = rows + QT
    value_t = v_ref[...].T
    for tile in range(rows // QT):
        start = tile * QT
        query = q_ref[pl.ds(start, QT), :] * jnp.asarray(HD**-0.5, BF)
        keys = k_ref[pl.ds(start, width), :]
        allowed = allowed_keys(lo_ref[:, start : start + QT], start, width, QT, rows)
        parts = []
        for head in range(2):
            query_h = jnp.where(head_lanes(query.shape, head), query, jnp.zeros_like(query))
            scores = jnp.where(allowed, nt(keys, query_h), MASKED)
            peak = jnp.max(scores, axis=0, keepdims=True)
            expo = jnp.exp(scores - peak)
            total = jnp.sum(expo, axis=0, keepdims=True)
            attend = (expo * (1.0 / total)).astype(BF)
            parts.append(
                nn(value_t[head * HD : (head + 1) * HD, start : start + width], attend)
            )
            lse_ref[0, head : head + 1, start : start + QT] = peak + jnp.log(total)
        ctx_ref[pl.ds(start, QT), :] = jnp.concatenate(parts, axis=0).T.astype(BF)


def attend_backward(
    lo_ref, q_ref, k_ref, v_ref, ctx_ref, lse_ref, grad_ref, dq_ref, dk_ref, dv_ref, dk_acc, dv_acc
):
    rows = q_ref.shape[0]
    width = rows + QT
    scale = HD**-0.5
    dk_acc[...] = jnp.zeros_like(dk_acc)
    dv_acc[...] = jnp.zeros_like(dv_acc)
    key_t = k_ref[...].T
    for tile in range(rows // QT):
        start = tile * QT
        query = q_ref[pl.ds(start, QT), :] * jnp.asarray(scale, BF)
        grad = grad_ref[pl.ds(start, QT), :]
        keys = k_ref[pl.ds(start, width), :]
        values = v_ref[pl.ds(start, width), :]
        allowed = allowed_keys(lo_ref[:, start : start + QT], start, width, QT, rows)
        inner_t = (grad.astype(F32) * ctx_ref[pl.ds(start, QT), :].astype(F32)).T
        parts = []
        dk_sum, dv_sum = None, None
        for head in range(2):
            lanes = head_lanes(query.shape, head)
            query_h = jnp.where(lanes, query, jnp.zeros_like(query))
            grad_h = jnp.where(lanes, grad, jnp.zeros_like(grad))
            scores = jnp.where(allowed, nt(keys, query_h), MASKED)
            attend = jnp.exp(scores - lse_ref[0, head : head + 1, start : start + QT])
            inner = jnp.sum(inner_t[head * HD : (head + 1) * HD, :], axis=0, keepdims=True)
            dscores = (attend * (nt(values, grad_h) - inner)).astype(BF)
            dv_part = nn(attend.astype(BF), grad_h)
            dk_part = nn(dscores, query_h)
            dv_sum = dv_part if dv_sum is None else dv_sum + dv_part
            dk_sum = dk_part if dk_sum is None else dk_sum + dk_part
            parts.append(
                nn(key_t[head * HD : (head + 1) * HD, start : start + width], dscores) * scale
            )
        dq_ref[pl.ds(start, QT), :] = jnp.concatenate(parts, axis=0).T.astype(BF)
        dk_acc[pl.ds(start, width), :] += dk_sum
        dv_acc[pl.ds(start, width), :] += dv_sum
    dk_ref[...] = dk_acc[...].astype(BF)
    dv_ref[...] = dv_acc[...].astype(BF)


LANES = 2 * HD


def columns(rows, base=0):
    return pl.BlockSpec((rows, LANES), lambda pair: (0, pair + base))


def attention_forward(lo, queries, key_rows, values, part, parts):
    rows, width = queries.shape
    pairs = width // LANES // parts
    base = pairs * part
    return pl.pallas_call(
        attend_forward,
        grid=(pairs,),
        in_specs=[
            pl.BlockSpec((1, rows), lambda pair: (0, 0)),
            columns(rows, base),
            columns(2 * rows, base),
            columns(2 * rows, base),
        ],
        out_specs=[columns(rows), pl.BlockSpec((1, 2, rows), lambda pair: (pair, 0, 0))],
        out_shape=[
            jax.ShapeDtypeStruct((rows, pairs * LANES), BF),
            jax.ShapeDtypeStruct((pairs, 2, rows), F32),
        ],
        compiler_params=pltpu.CompilerParams(vmem_limit_bytes=40 * 2**20),
        name="attend_forward",
    )(lo, queries, key_rows, values)


def attention_backward(lo, queries, key_rows, values, context, lse, dcontext, part, parts):
    rows, width = queries.shape
    pairs = width // LANES // parts
    base = pairs * part
    return pl.pallas_call(
        attend_backward,
        grid=(pairs,),
        in_specs=[
            pl.BlockSpec((1, rows), lambda pair: (0, 0)),
            columns(rows, base),
            columns(2 * rows, base),
            columns(2 * rows, base),
            columns(rows),
            pl.BlockSpec((1, 2, rows), lambda pair: (pair, 0, 0)),
            columns(rows, base),
        ],
        out_specs=[columns(rows), columns(2 * rows), columns(2 * rows)],
        out_shape=[
            jax.ShapeDtypeStruct((rows, pairs * LANES), BF),
            jax.ShapeDtypeStruct((2 * rows, pairs * LANES), BF),
            jax.ShapeDtypeStruct((2 * rows, pairs * LANES), BF),
        ],
        scratch_shapes=[
            pltpu.VMEM((2 * rows, LANES), F32),
            pltpu.VMEM((2 * rows, LANES), F32),
        ],
        compiler_params=pltpu.CompilerParams(vmem_limit_bytes=40 * 2**20),
        name="attend_backward",
    )(lo, queries, key_rows, values, context, lse, dcontext)


HIDDEN_TILE = 512
GELU_C = 0.7978845608028654
GELU_A = 0.044715


def up_body(x_ref, low_ref, high_ref, shift_ref, hidden_ref, slope_ref):
    half = low_ref.shape[0]
    v = nn(x_ref[:, :half], low_ref[...]) + nn(x_ref[:, half:], high_ref[...]) + shift_ref[...]
    square = v * v
    t = jnp.tanh(GELU_C * v * (1.0 + GELU_A * square))
    gate = 0.5 * (1.0 + t)
    hidden_ref[...] = (v * gate).astype(BF)
    slope = gate + (0.5 * GELU_C) * v * (1.0 - t * t) * (1.0 + (3.0 * GELU_A) * square)
    slope_ref[...] = slope.astype(BF)


def down_body(x_ref, low_ref, high_ref, slope_ref, dpre_ref, sum_ref):
    half = low_ref.shape[0]
    v = nn(x_ref[:, :half], low_ref[...]) + nn(x_ref[:, half:], high_ref[...])
    dpre = (v * slope_ref[...].astype(F32)).astype(BF)
    dpre_ref[...] = dpre
    sum_ref[...] = jnp.sum(dpre.astype(F32), axis=0, keepdims=True)


def mlp_call(body, name, x, low, high, side, outs):
    rows, width = x.shape
    hidden = low.shape[1]

    def tile(height):
        return pl.BlockSpec((height, HIDDEN_TILE), lambda j: (0, j))

    return pl.pallas_call(
        body,
        grid=(hidden // HIDDEN_TILE,),
        in_specs=[
            pl.BlockSpec((rows, width), lambda j: (0, 0)),
            tile(low.shape[0]),
            tile(high.shape[0]),
            tile(side.shape[0]),
        ],
        out_specs=[tile(height) for height, _ in outs],
        out_shape=[jax.ShapeDtypeStruct((height, hidden), kind) for height, kind in outs],
        compiler_params=pltpu.CompilerParams(vmem_limit_bytes=40 * 2**20),
        name=name,
    )(x, low, high, side)


def lowest_keys(lengths, rows):
    count = lengths.shape[0]
    step = jnp.arange(count, dtype=jnp.int32)
    ends = jnp.sum(jnp.where(step[None, :] <= step[:, None], lengths[None, :], 0), axis=1)
    base = lax.axis_index("tp") * rows
    places = base + jnp.arange(rows, dtype=jnp.int32)
    begins = jnp.max(jnp.where(ends[:, None] <= places[None, :], ends[:, None], 0), axis=0)
    return (begins - base + rows).astype(jnp.int32)[None, :]


def per_device(
    inputs,
    seq_lengths,
    qkv_w,
    out_w,
    fc_w,
    proj_w,
    ln1_gain,
    ln1_bias,
    q_bias,
    v_bias,
    out_bias,
    ln2_gain,
    ln2_bias,
    fc_bias,
    proj_bias,
    cotangent,
):
    rows = inputs.shape[0]
    half = inputs.shape[1] // 2
    tp_size = lax.axis_size("tp")
    masks = step_masks()
    blocks = slot_blocks()
    exchanged = [True, True, False, False, True, True, True, False, True]

    def dot(left, right):
        return jnp.dot(left, right, preferred_element_type=F32)

    def dot_nt(left, right):
        return jnp.einsum("rj,ij->ri", left, right, preferred_element_type=F32)

    def dot_tn(left, right):
        return jnp.einsum("ri,rj->ij", left, right, preferred_element_type=F32).astype(BF)

    def dot_halves(left, low, high):
        return dot(left[:, :half], low) + dot(left[:, half:], high)

    def wide_nt(left, low, high):
        return jnp.concatenate([dot_nt(left, low), dot_nt(left, high)], axis=1)

    attn_part = jnp.concatenate([qkv_w, out_w.T[None]], axis=0)
    proj_part = proj_w.T[None]
    attn_slab = gather_tp(attn_part)
    (
        gain_one,
        shift_one,
        query_shift,
        value_shift,
        attn_shift,
        gain_two,
        shift_two,
        hidden_shift,
        mlp_shift,
    ) = gather_vectors(
        [ln1_gain, ln1_bias, q_bias, v_bias, out_bias, ln2_gain, ln2_bias, fc_bias, proj_bias],
        exchanged,
        blocks,
    )
    own = reorder(inputs, blocks)
    cot = reorder(cotangent, blocks)
    lo = lowest_keys(seq_lengths[0], rows)

    attn_slab, own, fc_w = join(attn_slab, own, fc_w)
    before = lax.ppermute(own, "tp", [(i, i + 1) for i in range(tp_size - 1)])
    fc_slab = gather_tp(fc_w[None])
    attn_held = gather_step(attn_slab, masks[:-1])
    attn_low = gather_step(attn_held, masks[-1:])

    attn_low, fc_slab, proj_part, before = join(attn_low, fc_slab, proj_part, before)
    proj_slab = gather_tp(proj_part)
    attn_high = exchange(attn_low, "fsdp", 1)
    fc_held = gather_step(fc_slab, masks[:-1])
    residual = own.astype(F32)
    first_f, pull_one = jax.vjp(layer_norm, residual, gain_one[0], shift_one[0])
    first = first_f.astype(BF)
    first_before = layer_norm(before.astype(F32), gain_one, shift_one).astype(BF)
    first_both = jnp.concatenate([first_before, first], axis=0)

    attn_high, fc_held, first, first_both = join(attn_high, fc_held, first, first_both)
    fc_low = gather_step(fc_held, masks[-1:])
    queries = (dot_halves(first, attn_low[0], attn_high[0]) + query_shift).astype(BF)
    key_rows = dot_halves(first_both, attn_low[1], attn_high[1]).astype(BF)
    values = (dot_halves(first_both, attn_low[2], attn_high[2]) + value_shift).astype(BF)
    context_a, lse_a = attention_forward(lo, queries, key_rows, values, 0, 2)

    fc_low, proj_slab, context_a, queries, key_rows, values = join(
        fc_low, proj_slab, context_a, queries, key_rows, values
    )
    fc_high = exchange(fc_low, "fsdp", 1)
    proj_held = gather_step(proj_slab, masks[:-1])
    context_b, lse_b = attention_forward(lo, queries, key_rows, values, 1, 2)

    fc_high, proj_held, context_b = join(fc_high, proj_held, context_b)
    proj_low = gather_step(proj_held, masks[-1:])
    context = jnp.concatenate([context_a, context_b], axis=1)
    out_low, out_high = attn_low[3], attn_high[3]
    middle = residual + wide_nt(context, out_low, out_high) + attn_shift
    second_f, pull_two = jax.vjp(layer_norm, middle, gain_two[0], shift_two[0])
    second = second_f.astype(BF)
    hidden, slope = mlp_call(
        up_body, "mlp_up", second, fc_low[0], fc_high[0], hidden_shift, [(rows, BF), (rows, BF)]
    )

    proj_low, hidden, slope, cot, second = join(proj_low, hidden, slope, cot, second)
    proj_high = exchange(proj_low, "fsdp", 1)
    dproj_low = dot_tn(cot[:, :half], hidden)[None]
    dproj_high = dot_tn(cot[:, half:], hidden)[None]

    proj_high, dproj_low, dproj_high = join(proj_high, dproj_low, dproj_high)
    dproj_keep, dproj_send = scatter_core(dproj_low, dproj_high)
    dpre, dhidden_bias = mlp_call(
        down_body, "mlp_down", cot, proj_low[0], proj_high[0], slope, [(rows, BF), (1, F32)]
    )
    dfc_low = dot_tn(second[:, :half], dpre)[None]
    dfc_high = dot_tn(second[:, half:], dpre)[None]

    dproj_keep, dproj_send, dpre, dfc_low, dfc_high = join(
        dproj_keep, dproj_send, dpre, dfc_low, dfc_high
    )
    dproj_keep, dproj_got = scatter_step(dproj_keep, dproj_send, masks[-1:])
    dfc_keep, dfc_send = scatter_core(dfc_low, dfc_high)
    dsecond = wide_nt(dpre, fc_low[0], fc_high[0])
    dmiddle_norm, dgain_two, dshift_two = pull_two(dsecond)
    dmiddle = cot.astype(F32) + dmiddle_norm
    dattn = dmiddle.astype(BF)
    dcontext = dot_halves(dattn, out_low, out_high).astype(BF)
    dqueries_a, dkeys_a, dvalues_a = attention_backward(
        lo, queries, key_rows, values, context_a, lse_a, dcontext, 0, 2
    )

    dproj_keep, dproj_got, dfc_keep, dfc_send, dcontext, dqueries_a = join(
        dproj_keep, dproj_got, dfc_keep, dfc_send, dcontext, dqueries_a
    )
    dproj_keep, dproj_send = halves(dproj_keep, dproj_got)
    dproj_slab = add_low(*scatter_step(dproj_keep, dproj_send, masks[:-1][::-1]))
    dqueries_b, dkeys_b, dvalues_b = attention_backward(
        lo, queries, key_rows, values, context_b, lse_b, dcontext, 1, 2
    )
    dqueries = jnp.concatenate([dqueries_a, dqueries_b], axis=1)
    dkeys = jnp.concatenate([dkeys_a, dkeys_b], axis=1)
    dvalues = jnp.concatenate([dvalues_a, dvalues_b], axis=1)

    dproj_slab, dfc_keep, dfc_send, dqueries, dkeys, dvalues = join(
        dproj_slab, dfc_keep, dfc_send, dqueries, dkeys, dvalues
    )
    dfc_keep, dfc_got = scatter_step(dfc_keep, dfc_send, masks[-1:])
    dproj_w = scatter_tp(dproj_slab)
    low_rows = [dot_tn(first[:, :half], dqueries), dot_tn(first_both[:, :half], dkeys)]
    low_rows += [dot_tn(first_both[:, :half], dvalues), dot_tn(dattn[:, :half], context)]
    high_rows = [dot_tn(first[:, half:], dqueries), dot_tn(first_both[:, half:], dkeys)]
    high_rows += [dot_tn(first_both[:, half:], dvalues), dot_tn(dattn[:, half:], context)]
    dattn_low, dattn_high = jnp.stack(low_rows), jnp.stack(high_rows)

    dfc_keep, dfc_got, dattn_low, dattn_high, dproj_w, dkeys = join(
        dfc_keep, dfc_got, dattn_low, dattn_high, dproj_w, dkeys
    )
    dfc_keep, dfc_send = halves(dfc_keep, dfc_got)
    dfc_slab = add_low(*scatter_step(dfc_keep, dfc_send, masks[:-1][::-1]))
    dattn_keep, dattn_send = scatter_core(dattn_low, dattn_high)
    dfirst_both = wide_nt(dkeys, attn_low[1], attn_high[1]) + wide_nt(
        dvalues, attn_low[2], attn_high[2]
    )
    dfirst_own = dfirst_both[rows:] + wide_nt(dqueries, attn_low[0], attn_high[0])
    dfirst_send = dfirst_both[:rows].astype(BF)

    dfc_slab, dattn_keep, dattn_send, dfirst_own, dfirst_send, hidden = join(
        dfc_slab, dattn_keep, dattn_send, dfirst_own, dfirst_send, hidden
    )
    dattn_keep, dattn_got = scatter_step(dattn_keep, dattn_send, masks[-1:])
    dfirst_after = lax.ppermute(dfirst_send, "tp", [(i + 1, i) for i in range(tp_size - 1)])
    dfc_w = scatter_tp(dfc_slab)
    outputs = middle + wide_nt(hidden, proj_low[0], proj_high[0]) + mlp_shift
    outputs = reorder(outputs, blocks, back=True)

    dattn_keep, dattn_got, dfirst_after, outputs, dfc_w = join(
        dattn_keep, dattn_got, dfirst_after, outputs, dfc_w
    )
    dattn_keep, dattn_send = halves(dattn_keep, dattn_got)
    dattn_slab = add_low(*scatter_step(dattn_keep, dattn_send, masks[:-1][::-1]))
    dresidual, dgain_one, dshift_one = pull_one(dfirst_own + dfirst_after.astype(F32))
    dinputs = reorder(dmiddle + dresidual, blocks, back=True)
    vector_grads = scatter_vectors(
        [
            dgain_one,
            dshift_one,
            jnp.sum(dqueries, axis=0, dtype=F32),
            jnp.sum(dvalues, axis=0, dtype=F32),
            jnp.sum(dattn, axis=0, dtype=F32),
            dgain_two,
            dshift_two,
            dhidden_bias[0],
            jnp.sum(cot, axis=0, dtype=F32),
        ],
        exchanged,
        blocks,
    )
    dattn_w = scatter_tp(dattn_slab)
    return (
        outputs,
        dinputs,
        dattn_w[:3],
        dattn_w[3].T,
        dfc_w[0],
        dproj_w[0].T,
        *vector_grads,
    )


def solution(mesh):
    vector = P(("fsdp", "tp"))
    tokens = P(("fsdp", "tp"), None)
    weights = (P(None, "fsdp", "tp"), P("tp", "fsdp"), P("fsdp", "tp"), P("tp", "fsdp"))
    return jax.shard_map(
        per_device,
        mesh=mesh,
        in_specs=(tokens, P("fsdp", None), *weights, *([vector] * 9), tokens),
        out_specs=(tokens, tokens, *weights, *([vector] * 9)),
        check_vma=False,
    )
```

```python
import jax
import jax.numpy as jnp
from jax import lax
import numpy as np
from jax.experimental import pallas as pl
from jax.experimental.pallas import tpu as pltpu
from jax.sharding import PartitionSpec as P

HD = 64
QT = 256
EPSILON = 1e-05
MASKED = -1e30
BF = jnp.bfloat16
F32 = jnp.float32


def layer_norm(values, gain, shift):
    center = jnp.mean(values, axis=-1, keepdims=True)
    offset = values - center
    spread = jnp.mean(offset * offset, axis=-1, keepdims=True)
    return offset * lax.rsqrt(spread + EPSILON) * gain + shift


def gelu(values):
    return jax.nn.gelu(values, approximate=True)


def exchange(item, axis, mask):
    size = lax.axis_size(axis)
    return lax.ppermute(item, axis, [(i, i ^ mask) for i in range(size)])


def exchange_by_core(item, even_mask, odd_mask):
    size = lax.axis_size("fsdp")
    pairs = [(i, i ^ (odd_mask if i % 2 else even_mask)) for i in range(size)]
    return lax.ppermute(item, "fsdp", pairs)


def rotate(item, step):
    size = lax.axis_size("tp")
    return lax.ppermute(item, "tp", [(i, (i + step) % size) for i in range(size)])


def step_masks():
    bits = [1 << b for b in range(1, lax.axis_size("fsdp").bit_length() - 1)]
    return list(zip(bits, bits[::-1]))


def slot_blocks():
    held = [(0, 0)]
    for even, odd in step_masks():
        held = held + [(a ^ even, b ^ odd) for a, b in held]
    held = held + [(b ^ 1, a ^ 1) for a, b in held]
    table = np.asarray(held, np.int32)
    mine = lax.axis_index("fsdp")
    return mine ^ jnp.where(mine % 2 == 0, table[:, 0], table[:, 1])


def rotations(part):
    return [rotate(part, k) for k in range(1, lax.axis_size("tp"))]


def assemble_tp(part, got):
    size = lax.axis_size("tp")
    mine = lax.axis_index("tp")
    return jnp.concatenate(
        [lax.select_n((mine - p) % size, part, *got) for p in range(size)], axis=-1
    )


def grow(held, got):
    return jnp.concatenate([held, got], axis=1)


def gather_raw(held, masks):
    for even, odd in masks[:-1]:
        held = grow(held, exchange_by_core(held, even, odd))
    return held, exchange_by_core(held, *masks[-1])


def add_low(left, right):
    return (left.astype(F32) + right.astype(F32)).astype(BF)


def split_add(left, right):
    half = left.shape[1] // 2
    return (
        add_low(left[:, :half], right[:, :half]),
        add_low(left[:, half:], right[:, half:]),
    )


def scatter_raw(keep, send, masks):
    for even, odd in masks[:-1]:
        keep, send = split_add(keep, exchange_by_core(send, even, odd))
    return keep, exchange_by_core(send, *masks[-1])


def core_swap(item):
    return exchange(item, "fsdp", 1)


def scatter_tp_raw(slab):
    size = lax.axis_size("tp")
    mine = lax.axis_index("tp")
    cols = slab.shape[-1] // size
    parts = [slab[:, :, p * cols : (p + 1) * cols] for p in range(size)]
    got = [rotate(lax.select_n((mine + k) % size, *parts), k) for k in range(1, size)]
    return [lax.select_n(mine, *parts), *got]


def total_tp(parts):
    total = parts[0].astype(F32)
    for part in parts[1:]:
        total = total + part.astype(F32)
    return total


def join(*items):
    return jax.tree.unflatten(
        jax.tree.structure(items), lax.optimization_barrier(tuple(jax.tree.leaves(items)))
    )


def pick(items, order):
    slot = jnp.arange(items.shape[0], dtype=jnp.int32)
    chosen = (order[:, None] == slot[None, :]).reshape(
        (items.shape[0],) * 2 + (1,) * (items.ndim - 1)
    )
    return jnp.sum(jnp.where(chosen, items[None], jnp.zeros_like(items)[None]), axis=1).astype(
        items.dtype
    )


def inverse(blocks):
    slot = jnp.arange(blocks.shape[0], dtype=jnp.int32)
    return jnp.sum(jnp.where(blocks[None, :] == slot[:, None], slot[None, :], 0), axis=1)


def reorder(values, blocks, back=False):
    rows, width = values.shape
    count = blocks.shape[0]
    lanes = width // count
    if lanes % 128:
        order = inverse(blocks) if back else blocks
        split = pick(values.reshape(rows, count, lanes).swapaxes(0, 1), order)
        return split.swapaxes(0, 1).reshape(rows, width)

    def body(table, source, target):
        for j in range(count):
            moved = pl.ds(pl.multiple_of(table[j] * lanes, lanes), lanes)
            plain = pl.ds(j * lanes, lanes)
            if back:
                target[:, moved] = source[:, plain]
            else:
                target[:, plain] = source[:, moved]

    tile = pl.BlockSpec((rows // 4, width), lambda i: (i, 0))
    return pl.pallas_call(
        body,
        grid=(4,),
        in_specs=[pl.BlockSpec(memory_space=pltpu.SMEM), tile],
        out_specs=tile,
        out_shape=jax.ShapeDtypeStruct(values.shape, values.dtype),
        name="reorder",
    )(blocks, values)


def gather_vectors(vectors, which, blocks):
    pack = jnp.concatenate(vectors)[None, None]
    size = lax.axis_size("tp")
    mine = lax.axis_index("tp")
    got = [pack] + [rotate(pack, k) for k in range(1, size)]
    pack = jnp.concatenate(
        [lax.select_n((mine - p) % size, *got) for p in range(size)], axis=1
    )
    where = lax.axis_index("fsdp")
    for b in range(lax.axis_size("fsdp").bit_length() - 1):
        other = exchange(pack, "fsdp", 1 << b)
        high = (where >> b) % 2 == 1
        pack = jnp.concatenate(
            [jnp.where(high, other, pack), jnp.where(high, pack, other)], axis=0
        )
    moved = pick(pack, blocks)
    out, at = [], 0
    for item, exchanged in zip(vectors, which):
        source = moved if exchanged else pack
        out.append(source[:, :, at : at + item.shape[0]].reshape(1, -1).astype(F32))
        at += item.shape[0]
    return out


def pack_vectors(vectors, which, blocks):
    count = lax.axis_size("fsdp")
    size = lax.axis_size("tp")
    packs = [
        jnp.concatenate(
            [v.reshape(count, size, -1) for v, m in zip(vectors, which) if m == kind], axis=2
        )
        for kind in (True, False)
    ]
    return jnp.concatenate([pick(packs[0], inverse(blocks)), packs[1]], axis=2)


def scatter_pack(pack, bits):
    where = lax.axis_index("fsdp")
    for b in bits:
        half = pack.shape[0] // 2
        high = (where >> b) % 2 == 1
        low_part, high_part = pack[:half], pack[half:]
        keep = jnp.where(high, high_part, low_part)
        send = jnp.where(high, low_part, high_part)
        pack = keep + exchange(send, "fsdp", 1 << b)
    return pack


def unpack_vectors(pack, lengths, which):
    mine = lax.axis_index("tp")
    size = lax.axis_size("tp")
    rows = [pack[0, p] for p in range(size)]
    total = lax.select_n(mine, *rows)
    for k in range(1, size):
        total = total + rotate(lax.select_n((mine + k) % size, *rows), k)
    out, at = {}, 0
    for kind in (True, False):
        for i, length in enumerate(lengths):
            if which[i] == kind:
                out[i] = total[at : at + length]
                at += length
    return [out[i] for i in range(len(lengths))]


def head_lanes(shape, head):
    lane = lax.broadcasted_iota(jnp.int32, shape, 1)
    return (lane >= head * HD) & (lane < (head + 1) * HD)


def nt(left, right):
    return lax.dot_general(left, right, (((1,), (1,)), ((), ())), preferred_element_type=F32)


def nn(left, right):
    return lax.dot_general(left, right, (((1,), (0,)), ((), ())), preferred_element_type=F32)


def allowed_keys(lo_row, start, keys, queries, rows):
    key = start + lax.broadcasted_iota(jnp.int32, (keys, queries), 0)
    query = rows + start + lax.broadcasted_iota(jnp.int32, (keys, queries), 1)
    return (key >= lo_row) & (key <= query)


def attend_forward(lo_ref, q_ref, k_ref, v_ref, *refs):
    ctx_ref, lse_ref = refs[-2:]
    rows = q_ref.shape[0]
    width = rows + QT
    value_t = v_ref[...].T
    for tile in range(rows // QT):
        start = tile * QT
        query = q_ref[pl.ds(start, QT), :] * jnp.asarray(HD**-0.5, BF)
        keys = k_ref[pl.ds(start, width), :]
        allowed = allowed_keys(lo_ref[:, start : start + QT], start, width, QT, rows)
        parts = []
        for head in range(2):
            query_h = jnp.where(head_lanes(query.shape, head), query, jnp.zeros_like(query))
            scores = jnp.where(allowed, nt(keys, query_h), MASKED)
            peak = jnp.max(scores, axis=0, keepdims=True)
            expo = jnp.exp(scores - peak)
            total = jnp.sum(expo, axis=0, keepdims=True)
            attend = (expo * (1.0 / total)).astype(BF)
            parts.append(
                nn(value_t[head * HD : (head + 1) * HD, start : start + width], attend)
            )
            lse_ref[0, head : head + 1, start : start + QT] = peak + jnp.log(total)
        ctx_ref[pl.ds(start, QT), :] = jnp.concatenate(parts, axis=0).T.astype(BF)


def attend_backward(lo_ref, q_ref, k_ref, v_ref, ctx_ref, lse_ref, grad_ref, *refs):
    out_ref, dk_acc, dv_acc = refs[-3:]
    rows = q_ref.shape[0]
    width = rows + QT
    scale = HD**-0.5
    dk_acc[...] = jnp.zeros_like(dk_acc)
    dv_acc[...] = jnp.zeros_like(dv_acc)
    key_t = k_ref[...].T
    for tile in range(rows // QT):
        start = tile * QT
        query = q_ref[pl.ds(start, QT), :] * jnp.asarray(scale, BF)
        grad = grad_ref[pl.ds(start, QT), :]
        keys = k_ref[pl.ds(start, width), :]
        values = v_ref[pl.ds(start, width), :]
        allowed = allowed_keys(lo_ref[:, start : start + QT], start, width, QT, rows)
        inner_t = (grad.astype(F32) * ctx_ref[pl.ds(start, QT), :].astype(F32)).T
        parts = []
        dk_sum, dv_sum = None, None
        for head in range(2):
            lanes = head_lanes(query.shape, head)
            query_h = jnp.where(lanes, query, jnp.zeros_like(query))
            grad_h = jnp.where(lanes, grad, jnp.zeros_like(grad))
            scores = jnp.where(allowed, nt(keys, query_h), MASKED)
            attend = jnp.exp(scores - lse_ref[0, head : head + 1, start : start + QT])
            inner = jnp.sum(inner_t[head * HD : (head + 1) * HD, :], axis=0, keepdims=True)
            dscores = (attend * (nt(values, grad_h) - inner)).astype(BF)
            dv_part = nn(attend.astype(BF), grad_h)
            dk_part = nn(dscores, query_h)
            dv_sum = dv_part if dv_sum is None else dv_sum + dv_part
            dk_sum = dk_part if dk_sum is None else dk_sum + dk_part
            parts.append(
                nn(key_t[head * HD : (head + 1) * HD, start : start + width], dscores) * scale
            )
        out_ref[0, pl.ds(rows + start, QT), :] = jnp.concatenate(parts, axis=0).T.astype(BF)
        dk_acc[pl.ds(start, width), :] += dk_sum
        dv_acc[pl.ds(start, width), :] += dv_sum
    out_ref[0, pl.ds(0, rows), :] = jnp.zeros((rows, out_ref.shape[2]), BF)
    out_ref[1] = dk_acc[...].astype(BF)
    out_ref[2] = dv_acc[...].astype(BF)


LANES = 2 * HD


def attention_specs(rows, base):
    def projected(kind, height, block):
        return pl.BlockSpec((None, height, LANES), lambda pair: (kind, block, pair + base))

    return [
        pl.BlockSpec((1, rows), lambda pair: (0, 0)),
        projected(0, rows, 1),
        projected(1, 2 * rows, 0),
        projected(2, 2 * rows, 0),
    ]


def attention_forward(lo, qkv, part=0, parts=1, into=()):
    rows, width = qkv.shape[1] // 2, qkv.shape[2]
    pairs = width // LANES // parts
    base = pairs * part
    return pl.pallas_call(
        attend_forward,
        grid=(pairs,),
        in_specs=attention_specs(rows, base)
        + [pl.BlockSpec(memory_space=pl.ANY) for _ in into],
        out_specs=[
            pl.BlockSpec((rows, LANES), lambda pair: (0, pair + base)),
            pl.BlockSpec((1, 2, rows), lambda pair: (pair + base, 0, 0)),
        ],
        out_shape=[
            jax.ShapeDtypeStruct((rows, width), BF),
            jax.ShapeDtypeStruct((width // LANES, 2, rows), F32),
        ],
        input_output_aliases={4 + i: i for i in range(len(into))},
        compiler_params=pltpu.CompilerParams(vmem_limit_bytes=40 * 2**20),
        name="attend_forward",
    )(lo, qkv, qkv, qkv, *into)


def attention_backward(lo, qkv, context, lse, dcontext, part=0, parts=1, into=()):
    rows, width = qkv.shape[1] // 2, qkv.shape[2]
    pairs = width // LANES // parts
    base = pairs * part
    tokens = pl.BlockSpec((rows, LANES), lambda pair: (0, pair + base))
    return pl.pallas_call(
        attend_backward,
        grid=(pairs,),
        in_specs=attention_specs(rows, base)
        + [tokens, pl.BlockSpec((1, 2, rows), lambda pair: (pair + base, 0, 0)), tokens]
        + [pl.BlockSpec(memory_space=pl.ANY) for _ in into],
        out_specs=pl.BlockSpec((3, 2 * rows, LANES), lambda pair: (0, 0, pair + base)),
        out_shape=jax.ShapeDtypeStruct(qkv.shape, BF),
        scratch_shapes=[
            pltpu.VMEM((2 * rows, LANES), F32),
            pltpu.VMEM((2 * rows, LANES), F32),
        ],
        input_output_aliases={7 + i: i for i in range(len(into))},
        compiler_params=pltpu.CompilerParams(vmem_limit_bytes=40 * 2**20),
        name="attend_backward",
    )(lo, qkv, qkv, qkv, context, lse, dcontext, *into)


def nn_pieces(x_ref, pieces):
    quarter = pieces[0].shape[0]
    weight = jnp.concatenate([piece[...] for piece in pieces], axis=0)
    return nn(x_ref[:, : 4 * quarter], weight)


def nt_pieces(grad, pieces):
    weight = jnp.concatenate([piece[...] for piece in pieces], axis=0)
    return nt(grad, weight)


def project_body(x_ref, *refs):
    pieces, shift_ref, out_ref = refs[:4], refs[4], refs[5]
    out_ref[...] = (nn_pieces(x_ref, pieces) + shift_ref[...]).astype(BF)


def project(x, pieces, shifts):
    rows, width = x.shape
    quarter, cols = pieces[0].shape[1:]
    tile = min(cols, 512)

    def part(height):
        return pl.BlockSpec((None, height, tile), lambda c, j: (c, 0, j))

    return pl.pallas_call(
        project_body,
        grid=(3, cols // tile),
        in_specs=[
            pl.BlockSpec((rows, width), lambda c, j: (0, 0)),
            *[part(quarter)] * 4,
            part(1),
        ],
        out_specs=part(rows),
        out_shape=jax.ShapeDtypeStruct((3, rows, cols), BF),
        compiler_params=pltpu.CompilerParams(vmem_limit_bytes=40 * 2**20),
        name="project",
    )(x, *pieces, shifts)


def project_back_body(grad_ref, *refs):
    pieces, (own_ref, send_ref, acc_ref) = refs[:4], refs[4:]
    kind = pl.program_id(0)
    rows = own_ref.shape[0]
    part = nt_pieces(grad_ref[...], pieces)

    @pl.when(kind == 0)
    def _():
        acc_ref[...] = part

    @pl.when(kind > 0)
    def _():
        acc_ref[...] += part

    @pl.when(kind == pl.num_programs(0) - 1)
    def _():
        send_ref[...] = acc_ref[:rows, :].astype(BF)
        own_ref[...] = acc_ref[rows:, :]


def project_back(grads, pieces):
    _, both, cols = grads.shape
    quarter = pieces[0].shape[1]
    rows = both // 2

    def part(height):
        return pl.BlockSpec((None, height, cols), lambda c: (c, 0, 0))

    whole = pl.BlockSpec((rows, 4 * quarter), lambda c: (0, 0))
    return pl.pallas_call(
        project_back_body,
        grid=(3,),
        in_specs=[part(both)] + [part(quarter)] * 4,
        out_specs=[whole, whole],
        out_shape=[
            jax.ShapeDtypeStruct((rows, 4 * quarter), F32),
            jax.ShapeDtypeStruct((rows, 4 * quarter), BF),
        ],
        scratch_shapes=[pltpu.VMEM((both, 4 * quarter), F32)],
        compiler_params=pltpu.CompilerParams(vmem_limit_bytes=40 * 2**20),
        name="project_back",
    )(grads, *pieces)


HIDDEN_TILE = 512
GELU_C = 0.7978845608028654
GELU_A = 0.044715


def up_body(x_ref, *refs):
    pieces, (shift_ref, hidden_ref, slope_ref) = refs[:4], refs[4:]
    v = nn_pieces(x_ref, pieces) + shift_ref[...]
    square = v * v
    t = jnp.tanh(GELU_C * v * (1.0 + GELU_A * square))
    gate = 0.5 * (1.0 + t)
    hidden_ref[...] = (v * gate).astype(BF)
    slope = gate + (0.5 * GELU_C) * v * (1.0 - t * t) * (1.0 + (3.0 * GELU_A) * square)
    slope_ref[...] = slope.astype(BF)


def down_body(x_ref, *refs):
    pieces, slope_ref, up_pieces = refs[:4], refs[4], refs[5:9]
    dpre_ref, sum_ref, dsecond_ref = refs[9:]
    v = nn_pieces(x_ref, pieces)
    dpre = (v * slope_ref[...].astype(F32)).astype(BF)
    dpre_ref[...] = dpre
    sum_ref[...] = jnp.sum(dpre.astype(F32), axis=0, keepdims=True)
    part = nt_pieces(dpre, up_pieces)

    @pl.when(pl.program_id(0) == 0)
    def _():
        dsecond_ref[...] = part

    @pl.when(pl.program_id(0) > 0)
    def _():
        dsecond_ref[...] += part


def hidden_tile(height):
    return pl.BlockSpec((height, HIDDEN_TILE), lambda j: (0, j))


def piece_tiles(pieces):
    return [
        pl.BlockSpec((None, piece.shape[1], HIDDEN_TILE), lambda j: (0, 0, j)) for piece in pieces
    ]


def mlp_up(x, pieces, shift):
    rows, width = x.shape
    hidden = shift.shape[1]
    return pl.pallas_call(
        up_body,
        grid=(hidden // HIDDEN_TILE,),
        in_specs=[pl.BlockSpec((rows, width), lambda j: (0, 0))]
        + piece_tiles(pieces)
        + [hidden_tile(1)],
        out_specs=[hidden_tile(rows), hidden_tile(rows)],
        out_shape=[jax.ShapeDtypeStruct((rows, hidden), BF)] * 2,
        compiler_params=pltpu.CompilerParams(vmem_limit_bytes=40 * 2**20),
        name="mlp_up",
    )(x, *pieces, shift)


def mlp_down(x, pieces, slope, up_pieces):
    rows, width = x.shape
    hidden = slope.shape[1]
    whole = pl.BlockSpec((rows, width), lambda j: (0, 0))
    return pl.pallas_call(
        down_body,
        grid=(hidden // HIDDEN_TILE,),
        in_specs=[whole] + piece_tiles(pieces) + [hidden_tile(rows)] + piece_tiles(up_pieces),
        out_specs=[hidden_tile(rows), hidden_tile(1), whole],
        out_shape=[
            jax.ShapeDtypeStruct((rows, hidden), BF),
            jax.ShapeDtypeStruct((1, hidden), F32),
            jax.ShapeDtypeStruct((rows, width), F32),
        ],
        compiler_params=pltpu.CompilerParams(vmem_limit_bytes=40 * 2**20),
        name="mlp_down",
    )(x, *pieces, slope, *up_pieces)


def grad_body(x_ref, y_ref, *refs):
    pieces, turned = refs[-5:-1], refs[-1]
    first = (pl.program_id(0) == 0) & (pl.program_id(1) == 0)

    @pl.when(first)
    def _():
        turned[...] = x_ref[...].T

    quarter = pieces[0].shape[0]
    y = y_ref[...]
    for i, piece in enumerate(pieces):
        piece[...] = nn(turned[i * quarter : (i + 1) * quarter, :], y).astype(BF)


def weight_grads(x, y, kinds=1, place=0, into=()):
    rows, width = x.shape
    count, _, cols = y.shape
    tile = 512
    piece = jax.ShapeDtypeStruct((kinds, width // 4, cols), BF)
    return pl.pallas_call(
        grad_body,
        grid=(count, cols // tile),
        in_specs=[
            pl.BlockSpec((rows, width), lambda c, j: (0, 0)),
            pl.BlockSpec((None, rows, tile), lambda c, j: (c, 0, j)),
        ]
        + [pl.BlockSpec(memory_space=pl.ANY) for _ in into],
        out_specs=[pl.BlockSpec((None, width // 4, tile), lambda c, j: (c + place, 0, j))] * 4,
        out_shape=[piece] * 4,
        scratch_shapes=[pltpu.VMEM((width, rows), BF)],
        input_output_aliases={2 + i: i for i in range(len(into))},
        compiler_params=pltpu.CompilerParams(vmem_limit_bytes=40 * 2**20),
        name="weight_grads",
    )(x, y, *into)


def out_body(table, x_ref, *refs):
    pieces, (middle_ref, shift_ref, out_ref, acc_ref) = refs[:4], refs[4:]
    step = pl.program_id(0)
    part = nt_pieces(x_ref[...], pieces)

    @pl.when(step == 0)
    def _():
        acc_ref[...] = part + middle_ref[...] + shift_ref[...]

    @pl.when(step > 0)
    def _():
        acc_ref[...] += part

    @pl.when(step == pl.num_programs(0) - 1)
    def _():
        lanes = out_ref.shape[1] // table.shape[0]
        for j in range(table.shape[0]):
            moved = pl.ds(pl.multiple_of(table[j] * lanes, lanes), lanes)
            out_ref[:, moved] = acc_ref[:, j * lanes : (j + 1) * lanes]


def mlp_out(hidden, pieces, middle, shift, blocks):
    rows, width = middle.shape
    moves = (width // blocks.shape[0]) % 128 == 0
    table = blocks if moves else jnp.zeros((1,), jnp.int32)
    whole = pl.BlockSpec((rows, width), lambda j: (0, 0))
    out = pl.pallas_call(
        out_body,
        grid=(hidden.shape[1] // HIDDEN_TILE,),
        in_specs=[pl.BlockSpec(memory_space=pltpu.SMEM), hidden_tile(rows)]
        + piece_tiles(pieces)
        + [whole, pl.BlockSpec((1, width), lambda j: (0, 0))],
        out_specs=whole,
        out_shape=jax.ShapeDtypeStruct((rows, width), F32),
        scratch_shapes=[pltpu.VMEM((rows, width), F32)],
        compiler_params=pltpu.CompilerParams(vmem_limit_bytes=40 * 2**20),
        name="mlp_out",
    )(table, hidden, *pieces, middle, shift)
    return out if moves else reorder(out, blocks, back=True)


def normalize_body(before_ref, own_ref, gain_ref, shift_ref, out_ref):
    for part, ref in enumerate((before_ref, own_ref)):
        values = layer_norm(ref[...].astype(F32), gain_ref[...], shift_ref[...])
        out_ref[part] = values.astype(BF)


def normalize_both(before, own, gain, shift):
    rows, width = own.shape
    tile = pl.BlockSpec((rows // 4, width), lambda i: (i, 0))
    vector = pl.BlockSpec((1, width), lambda i: (0, 0))
    out = pl.pallas_call(
        normalize_body,
        grid=(4,),
        in_specs=[tile, tile, vector, vector],
        out_specs=pl.BlockSpec((2, rows // 4, width), lambda i: (0, i, 0)),
        out_shape=jax.ShapeDtypeStruct((2, rows, width), BF),
        name="normalize",
    )(before, own, gain, shift)
    return out.reshape(2 * rows, width)


def lowest_keys(lengths, rows):
    count = lengths.shape[0]
    step = jnp.arange(count, dtype=jnp.int32)
    ends = jnp.sum(jnp.where(step[None, :] <= step[:, None], lengths[None, :], 0), axis=1)
    base = lax.axis_index("tp") * rows
    places = base + jnp.arange(rows, dtype=jnp.int32)
    begins = jnp.max(jnp.where(ends[:, None] <= places[None, :], ends[:, None], 0), axis=0)
    return (begins - base + rows).astype(jnp.int32)[None, :]


def per_device(
    inputs,
    seq_lengths,
    qkv_w,
    out_w,
    fc_w,
    proj_w,
    ln1_gain,
    ln1_bias,
    q_bias,
    v_bias,
    out_bias,
    ln2_gain,
    ln2_bias,
    fc_bias,
    proj_bias,
    cotangent,
):
    rows = inputs.shape[0]
    quarter = inputs.shape[1] // 4
    tp_size = lax.axis_size("tp")
    masks = step_masks()
    near, far = masks[:-1], masks[-1:]
    blocks = slot_blocks()
    exchanged = [True, True, False, False, True, True, True, False, True]
    shards = [v.shape[0] for v in (ln1_gain, ln1_bias, q_bias, v_bias, out_bias)]
    shards += [v.shape[0] for v in (ln2_gain, ln2_bias, fc_bias, proj_bias)]
    bits = list(range(lax.axis_size("fsdp").bit_length() - 1))[::-1]

    def dot_nt(left, right):
        return jnp.einsum("rj,ij->ri", left, right, preferred_element_type=F32)

    def wide_nt(left, pieces, kind=0):
        return jnp.concatenate([dot_nt(left, piece[kind]) for piece in pieces], axis=1)

    def dot_pieces(left, pieces, kind):
        return sum(
            jnp.dot(quarter_of(left, i), piece[kind], preferred_element_type=F32)
            for i, piece in enumerate(pieces)
        )

    def quarter_of(values, i):
        return values[:, i * quarter : (i + 1) * quarter]

    attn_part = jnp.concatenate([qkv_w, out_w.T[None]], axis=0)
    attn_got = rotations(attn_part)
    vectors = [ln1_gain, ln1_bias, q_bias, v_bias, out_bias]
    vectors += [ln2_gain, ln2_bias, fc_bias, proj_bias]
    inputs, attn_part, *vectors = join(inputs, attn_part, *vectors)
    own = reorder(inputs, blocks)
    before = lax.ppermute(own, "tp", [(i, i + 1) for i in range(tp_size - 1)])
    (
        gain_one,
        shift_one,
        query_shift,
        value_shift,
        attn_shift,
        gain_two,
        shift_two,
        hidden_shift,
        mlp_shift,
    ) = gather_vectors(vectors, exchanged, blocks)
    cot = reorder(cotangent, blocks)
    lo = lowest_keys(seq_lengths[0], rows)
    proj_part = proj_w.T[None]

    *attn_got, gain_one, before, own, cot, fc_part, proj_part = join(
        *attn_got, gain_one, before, own, cot, fc_w[None], proj_part
    )
    attn_held, attn_got = gather_raw(assemble_tp(attn_part, attn_got), near)
    fc_got = rotations(fc_part)

    attn_got, own, proj_part = join(attn_got, own, proj_part)
    attn_a, attn_b = gather_raw(grow(attn_held, attn_got), far)
    attn_c = core_swap(attn_a)
    first_both = normalize_both(before, own, gain_one, shift_one)

    attn_b, attn_c, *fc_got, proj_part, first_both = join(
        attn_b, attn_c, *fc_got, proj_part, first_both
    )
    attn_d = core_swap(attn_b)
    fc_slab = assemble_tp(fc_part, fc_got)

    attn_d, fc_slab, first_both = join(attn_d, fc_slab, first_both)
    attn = (attn_a, attn_b, attn_c, attn_d)
    fc_held, fc_step = gather_raw(fc_slab, near)
    shifts = jnp.stack([query_shift, jnp.zeros_like(query_shift), value_shift])
    qkv = project(first_both, attn, shifts)

    fc_step, qkv, proj_part = join(fc_step, qkv, proj_part)
    fc_a, fc_b = gather_raw(grow(fc_held, fc_step), far)
    fc_c = core_swap(fc_a)
    proj_got = rotations(proj_part)
    context, lse = attention_forward(lo, qkv)

    fc_b, fc_c, *proj_got, context = join(fc_b, fc_c, *proj_got, context)
    fc_d = core_swap(fc_b)
    proj_held, proj_step = gather_raw(assemble_tp(proj_part, proj_got), near)
    residual = own.astype(F32)
    middle = residual + wide_nt(context, attn, 3) + attn_shift
    second_f, pull_two = jax.vjp(layer_norm, middle, gain_two[0], shift_two[0])
    second = second_f.astype(BF)

    fc_d, proj_step, second = join(fc_d, proj_step, second)
    fc = (fc_a, fc_b, fc_c, fc_d)
    proj_a, proj_b = gather_raw(grow(proj_held, proj_step), far)
    proj_c = core_swap(proj_a)
    hidden, slope = mlp_up(second, fc, hidden_shift)

    proj_b, proj_c, hidden, slope, second = join(proj_b, proj_c, hidden, slope, second)
    proj_d = core_swap(proj_b)
    dproj = weight_grads(cot, hidden[None])
    dproj_got = [core_swap(dproj[3]), core_swap(dproj[2])]

    proj_d, *dproj_got, dproj = join(proj_d, *dproj_got, dproj)
    proj = (proj_a, proj_b, proj_c, proj_d)
    _, dproj_got[0] = scatter_raw(dproj[0], add_low(dproj[1], dproj_got[0]), far)
    dpre, dhidden_bias, dsecond = mlp_down(cot, proj, slope, fc)
    dfc = weight_grads(second, dpre[None])

    *dproj_got, dfc, dsecond = join(*dproj_got, dfc, dsecond)
    dfc_got = [core_swap(dfc[3]), core_swap(dfc[2])]
    dproj_keep = add_low(dproj[0], dproj_got[1])
    dproj_keep, dproj_got = scatter_raw(*split_add(dproj_keep, dproj_got[0]), near[::-1])
    dmiddle_norm, dgain_two, dshift_two = pull_two(dsecond)
    dmiddle = cot.astype(F32) + dmiddle_norm
    dattn = dmiddle.astype(BF)
    dcontext = dot_pieces(dattn, attn, 3).astype(BF)
    dout = weight_grads(dattn, context[None], kinds=4, place=3)

    dproj_got, dcontext, dout, dfc_got = join(dproj_got, dcontext, dout, dfc_got)
    _, dfc_got[0] = scatter_raw(dfc[0], add_low(dfc[1], dfc_got[0]), far)
    dproj_parts = scatter_tp_raw(add_low(dproj_keep, dproj_got))
    dqkv = attention_backward(lo, qkv, context, lse, dcontext)

    dfc_got, dproj_parts, dqkv = join(dfc_got, dproj_parts, dqkv)
    dfc_keep = add_low(dfc[0], dfc_got[1])
    dfc_keep, dfc_got = scatter_raw(*split_add(dfc_keep, dfc_got[0]), near[::-1])

    dattn_w = weight_grads(first_both, dqkv, kinds=4, into=tuple(dout))

    dfc_got, dattn_w, dqkv = join(dfc_got, dattn_w, dqkv)
    dattn_got = [core_swap(dattn_w[3]), core_swap(dattn_w[2])]
    dfc_parts = scatter_tp_raw(add_low(dfc_keep, dfc_got))
    dfirst_own, dfirst_send = project_back(dqkv, attn)

    dattn_got, dattn_w, dfirst_own, dfirst_send, hidden = join(
        dattn_got, dattn_w, dfirst_own, dfirst_send, hidden
    )
    _, dattn_got[0] = scatter_raw(dattn_w[0], add_low(dattn_w[1], dattn_got[0]), far)
    dfirst_after = lax.ppermute(dfirst_send, "tp", [(i + 1, i) for i in range(tp_size - 1)])
    outputs = mlp_out(hidden, proj, middle, mlp_shift, blocks)

    dattn_got, dfc_parts, dfirst_after, outputs, dfirst_own, dfirst_send, before = join(
        dattn_got, dfc_parts, dfirst_after, outputs, dfirst_own, dfirst_send, before
    )
    dattn_keep = add_low(dattn_w[0], dattn_got[1])
    dattn_keep, dattn_got = scatter_raw(*split_add(dattn_keep, dattn_got[0]), near[::-1])
    _, pull_one = jax.vjp(layer_norm, residual, gain_one[0], shift_one[0])
    dresidual, gain_own, shift_own = pull_one(dfirst_own + dfirst_after.astype(F32))
    vectors = pack_vectors(
        [
            gain_own,
            shift_own,
            jnp.sum(dqkv[0], axis=0, dtype=F32),
            jnp.sum(dqkv[2], axis=0, dtype=F32),
            jnp.sum(dattn, axis=0, dtype=F32),
            dgain_two,
            dshift_two,
            dhidden_bias[0],
            jnp.sum(cot, axis=0, dtype=F32),
        ],
        exchanged,
        blocks,
    )

    dattn_got, vectors, dresidual = join(dattn_got, vectors, dresidual)
    attn_parts = scatter_tp_raw(add_low(dattn_keep, dattn_got))
    vectors = scatter_pack(vectors, bits)
    dinputs = reorder(dmiddle + dresidual, blocks, back=True)
    vector_grads = unpack_vectors(vectors, shards, exchanged)
    attn_grad = total_tp(attn_parts)
    return (
        outputs,
        dinputs,
        attn_grad[:3],
        attn_grad[3].T,
        total_tp(dfc_parts)[0],
        total_tp(dproj_parts)[0].T,
        *vector_grads,
    )


def solution(mesh):
    vector = P(("fsdp", "tp"))
    tokens = P(("fsdp", "tp"), None)
    weights = (P(None, "fsdp", "tp"), P("tp", "fsdp"), P("fsdp", "tp"), P("tp", "fsdp"))
    return jax.shard_map(
        per_device,
        mesh=mesh,
        in_specs=(tokens, P("fsdp", None), *weights, *([vector] * 9), tokens),
        out_specs=(tokens, tokens, *weights, *([vector] * 9)),
        check_vma=False,
    )
```

```python
import jax
import jax.numpy as jnp
from jax import lax
import numpy as np
from jax.experimental import pallas as pl
from jax.experimental.pallas import tpu as pltpu
from jax.sharding import PartitionSpec as P

HD = 64
QT = 256
EPSILON = 1e-05
MASKED = -1e30
VMEM = 40 * 2**20
BF = jnp.bfloat16
F32 = jnp.float32


def layer_norm(values, gain, shift):
    center = jnp.mean(values, axis=-1, keepdims=True)
    offset = values - center
    spread = jnp.mean(offset * offset, axis=-1, keepdims=True)
    return offset * lax.rsqrt(spread + EPSILON) * gain + shift


def gelu(values):
    return jax.nn.gelu(values, approximate=True)


def exchange(item, axis, mask):
    size = lax.axis_size(axis)
    return lax.ppermute(item, axis, [(i, i ^ mask) for i in range(size)])


def exchange_by_core(item, even_mask, odd_mask):
    size = lax.axis_size("fsdp")
    pairs = [(i, i ^ (odd_mask if i % 2 else even_mask)) for i in range(size)]
    return lax.ppermute(item, "fsdp", pairs)


def rotate(item, step):
    size = lax.axis_size("tp")
    return lax.ppermute(item, "tp", [(i, (i + step) % size) for i in range(size)])


def step_masks():
    bits = [1 << b for b in range(1, lax.axis_size("fsdp").bit_length() - 1)]
    return list(zip(bits, bits[::-1]))


def slot_blocks():
    held = [(0, 0)]
    for even, odd in step_masks():
        held = held + [(a ^ even, b ^ odd) for a, b in held]
    held = held + [(b ^ 1, a ^ 1) for a, b in held]
    table = np.asarray(held, np.int32)
    mine = lax.axis_index("fsdp")
    return mine ^ jnp.where(mine % 2 == 0, table[:, 0], table[:, 1])


def rotations(part):
    return [rotate(part, k) for k in range(1, lax.axis_size("tp"))]


def assemble_tp(part, got):
    size = lax.axis_size("tp")
    mine = lax.axis_index("tp")
    return jnp.concatenate(
        [lax.select_n((mine - p) % size, part, *got) for p in range(size)], axis=-1
    )


def grow(held, got):
    return jnp.concatenate([held, got], axis=1)


def gather_raw(held, masks):
    for even, odd in masks[:-1]:
        held = grow(held, exchange_by_core(held, even, odd))
    held = lax.optimization_barrier(held)
    return held, exchange_by_core(held, *masks[-1])


def add_low(left, right):
    return (left.astype(F32) + right.astype(F32)).astype(BF)


def split_add(left, right):
    half = left.shape[1] // 2
    return (
        add_low(left[:, :half], right[:, :half]),
        add_low(left[:, half:], right[:, half:]),
    )


def scatter_raw(keep, send, masks):
    for even, odd in masks[:-1]:
        keep, send = split_add(keep, exchange_by_core(send, even, odd))
    return keep, exchange_by_core(send, *masks[-1])


def core_swap(item):
    return exchange(item, "fsdp", 1)


def scatter_tp_raw(slab):
    size = lax.axis_size("tp")
    mine = lax.axis_index("tp")
    cols = slab.shape[-1] // size
    parts = [slab[:, :, p * cols : (p + 1) * cols] for p in range(size)]
    got = [rotate(lax.select_n((mine + k) % size, *parts), k) for k in range(1, size)]
    return [lax.select_n(mine, *parts), *got]


def total_tp(parts):
    total = parts[0].astype(F32)
    for part in parts[1:]:
        total = total + part.astype(F32)
    return total


def join(*items):
    return jax.tree.unflatten(
        jax.tree.structure(items), lax.optimization_barrier(tuple(jax.tree.leaves(items)))
    )


def pick(items, order):
    slot = jnp.arange(items.shape[0], dtype=jnp.int32)
    chosen = (order[:, None] == slot[None, :]).reshape(
        (items.shape[0],) * 2 + (1,) * (items.ndim - 1)
    )
    return jnp.sum(jnp.where(chosen, items[None], jnp.zeros_like(items)[None]), axis=1).astype(
        items.dtype
    )


def inverse(blocks):
    slot = jnp.arange(blocks.shape[0], dtype=jnp.int32)
    return jnp.sum(jnp.where(blocks[None, :] == slot[:, None], slot[None, :], 0), axis=1)


def reorder(values, blocks, back=False):
    rows, width = values.shape
    count = blocks.shape[0]
    lanes = width // count
    if lanes % 128:
        order = inverse(blocks) if back else blocks
        split = pick(values.reshape(rows, count, lanes).swapaxes(0, 1), order)
        return split.swapaxes(0, 1).reshape(rows, width)

    def body(table, source, target):
        for j in range(count):
            moved = pl.ds(pl.multiple_of(table[j] * lanes, lanes), lanes)
            plain = pl.ds(j * lanes, lanes)
            if back:
                target[:, moved] = source[:, plain]
            else:
                target[:, plain] = source[:, moved]

    tile = pl.BlockSpec((rows // 4, width), lambda i: (i, 0))
    return pl.pallas_call(
        body,
        grid=(4,),
        in_specs=[pl.BlockSpec(memory_space=pltpu.SMEM), tile],
        out_specs=tile,
        out_shape=jax.ShapeDtypeStruct(values.shape, values.dtype),
        name="reorder",
    )(blocks, values)


def gather_vectors_fsdp(vectors):
    width = vectors[0].shape[0]
    pack = jnp.concatenate([v.reshape(1, 1, -1, width) for v in vectors], axis=2)
    where = lax.axis_index("fsdp")
    for b in range(lax.axis_size("fsdp").bit_length() - 1):
        other = exchange(pack, "fsdp", 1 << b)
        high = (where >> b) % 2 == 1
        pack = jnp.concatenate(
            [jnp.where(high, other, pack), jnp.where(high, pack, other)], axis=0
        )
    return pack


def spread_vectors(pack, got, lengths, which, blocks):
    size = lax.axis_size("tp")
    mine = lax.axis_index("tp")
    width = pack.shape[3]
    pack = jnp.concatenate(
        [lax.select_n((mine - p) % size, pack, *got) for p in range(size)], axis=1
    )
    moved = pick(pack, blocks)
    out, at = [], 0
    for length, exchanged in zip(lengths, which):
        source = moved if exchanged else pack
        count = length // width
        out.append(source[:, :, at : at + count].reshape(1, -1).astype(F32))
        at += count
    return out


def pack_vectors(vectors, which, blocks):
    count = lax.axis_size("fsdp")
    size = lax.axis_size("tp")
    packs = [
        jnp.concatenate(
            [v.reshape(count, size, -1) for v, m in zip(vectors, which) if m == kind], axis=2
        )
        for kind in (True, False)
    ]
    return jnp.concatenate([pick(packs[0], inverse(blocks)), packs[1]], axis=2)


def scatter_pack(pack, bits):
    where = lax.axis_index("fsdp")
    for b in bits:
        half = pack.shape[0] // 2
        high = (where >> b) % 2 == 1
        low_part, high_part = pack[:half], pack[half:]
        keep = jnp.where(high, high_part, low_part)
        send = jnp.where(high, low_part, high_part)
        pack = keep + exchange(send, "fsdp", 1 << b)
    return pack


def unpack_vectors(pack, lengths, which):
    mine = lax.axis_index("tp")
    size = lax.axis_size("tp")
    rows = [pack[0, p] for p in range(size)]
    total = lax.select_n(mine, *rows)
    for k in range(1, size):
        total = total + rotate(lax.select_n((mine + k) % size, *rows), k)
    out, at = {}, 0
    for kind in (True, False):
        for i, length in enumerate(lengths):
            if which[i] == kind:
                out[i] = total[at : at + length]
                at += length
    return [out[i] for i in range(len(lengths))]


def head_lanes(shape, head):
    lane = lax.broadcasted_iota(jnp.int32, shape, 1)
    return (lane >= head * HD) & (lane < (head + 1) * HD)


def nt(left, right):
    return lax.dot_general(left, right, (((1,), (1,)), ((), ())), preferred_element_type=F32)


def nn(left, right):
    return lax.dot_general(left, right, (((1,), (0,)), ((), ())), preferred_element_type=F32)


def allowed_keys(lo_row, start, keys, queries, rows):
    key = start + lax.broadcasted_iota(jnp.int32, (keys, queries), 0)
    query = rows + start + lax.broadcasted_iota(jnp.int32, (keys, queries), 1)
    return (key >= lo_row) & (key <= query)


def attend_forward(lo_ref, q_ref, k_ref, v_ref, *refs):
    ctx_ref, lse_ref = refs[-2:]
    rows = q_ref.shape[0]
    width = rows + QT
    value_t = v_ref[...].T
    for tile in range(rows // QT):
        start = tile * QT
        query = q_ref[pl.ds(start, QT), :] * jnp.asarray(HD**-0.5, BF)
        keys = k_ref[pl.ds(start, width), :]
        allowed = allowed_keys(lo_ref[:, start : start + QT], start, width, QT, rows)
        parts = []
        for head in range(2):
            query_h = jnp.where(head_lanes(query.shape, head), query, jnp.zeros_like(query))
            scores = jnp.where(allowed, nt(keys, query_h), MASKED)
            peak = jnp.max(scores, axis=0, keepdims=True)
            expo = jnp.exp(scores - peak)
            total = jnp.sum(expo, axis=0, keepdims=True)
            attend = expo.astype(BF)
            parts.append(
                nn(value_t[head * HD : (head + 1) * HD, start : start + width], attend)
                * (1.0 / total)
            )
            lse_ref[0, head : head + 1, start : start + QT] = peak + jnp.log(total)
        ctx_ref[pl.ds(start, QT), :] = jnp.concatenate(parts, axis=0).T.astype(BF)


def attend_backward(lo_ref, q_ref, k_ref, v_ref, ctx_ref, lse_ref, grad_ref, *refs):
    out_ref, dk_acc, dv_acc = refs[-3:]
    rows = q_ref.shape[0]
    width = rows + QT
    scale = HD**-0.5
    dk_acc[...] = jnp.zeros_like(dk_acc)
    dv_acc[...] = jnp.zeros_like(dv_acc)
    key_t = k_ref[...].T
    for tile in range(rows // QT):
        start = tile * QT
        query = q_ref[pl.ds(start, QT), :] * jnp.asarray(scale, BF)
        grad = grad_ref[pl.ds(start, QT), :]
        keys = k_ref[pl.ds(start, width), :]
        values = v_ref[pl.ds(start, width), :]
        allowed = allowed_keys(lo_ref[:, start : start + QT], start, width, QT, rows)
        inner_t = (grad.astype(F32) * ctx_ref[pl.ds(start, QT), :].astype(F32)).T
        parts = []
        dk_sum, dv_sum = None, None
        for head in range(2):
            lanes = head_lanes(query.shape, head)
            query_h = jnp.where(lanes, query, jnp.zeros_like(query))
            grad_h = jnp.where(lanes, grad, jnp.zeros_like(grad))
            scores = jnp.where(allowed, nt(keys, query_h), MASKED)
            attend = jnp.exp(scores - lse_ref[0, head : head + 1, start : start + QT])
            inner = jnp.sum(inner_t[head * HD : (head + 1) * HD, :], axis=0, keepdims=True)
            dscores = (attend * (nt(values, grad_h) - inner)).astype(BF)
            dv_part = nn(attend.astype(BF), grad_h)
            dk_part = nn(dscores, query_h)
            dv_sum = dv_part if dv_sum is None else dv_sum + dv_part
            dk_sum = dk_part if dk_sum is None else dk_sum + dk_part
            parts.append(
                nn(key_t[head * HD : (head + 1) * HD, start : start + width], dscores) * scale
            )
        out_ref[0, pl.ds(rows + start, QT), :] = jnp.concatenate(parts, axis=0).T.astype(BF)
        dk_acc[pl.ds(start, width), :] += dk_sum
        dv_acc[pl.ds(start, width), :] += dv_sum
    out_ref[0, pl.ds(0, rows), :] = jnp.zeros((rows, out_ref.shape[2]), BF)
    out_ref[1] = dk_acc[...].astype(BF)
    out_ref[2] = dv_acc[...].astype(BF)


LANES = 2 * HD


def attention_specs(rows, base):
    def projected(kind, height, block):
        return pl.BlockSpec((None, height, LANES), lambda pair: (kind, block, pair + base))

    return [
        pl.BlockSpec((1, rows), lambda pair: (0, 0)),
        projected(0, rows, 1),
        projected(1, 2 * rows, 0),
        projected(2, 2 * rows, 0),
    ]


def attention_forward(lo, qkv, part=0, parts=1, into=()):
    rows, width = qkv.shape[1] // 2, qkv.shape[2]
    pairs = width // LANES // parts
    base = pairs * part
    return pl.pallas_call(
        attend_forward,
        grid=(pairs,),
        in_specs=attention_specs(rows, base)
        + [pl.BlockSpec(memory_space=pl.ANY) for _ in into],
        out_specs=[
            pl.BlockSpec((rows, LANES), lambda pair: (0, pair + base)),
            pl.BlockSpec((1, 2, rows), lambda pair: (pair + base, 0, 0)),
        ],
        out_shape=[
            jax.ShapeDtypeStruct((rows, width), BF),
            jax.ShapeDtypeStruct((width // LANES, 2, rows), F32),
        ],
        input_output_aliases={4 + i: i for i in range(len(into))},
        compiler_params=pltpu.CompilerParams(vmem_limit_bytes=VMEM),
        name="attend_forward",
    )(lo, qkv, qkv, qkv, *into)


def attention_backward(lo, qkv, context, lse, dcontext, part=0, parts=1, into=()):
    rows, width = qkv.shape[1] // 2, qkv.shape[2]
    pairs = width // LANES // parts
    base = pairs * part
    tokens = pl.BlockSpec((rows, LANES), lambda pair: (0, pair + base))
    return pl.pallas_call(
        attend_backward,
        grid=(pairs,),
        in_specs=attention_specs(rows, base)
        + [tokens, pl.BlockSpec((1, 2, rows), lambda pair: (pair + base, 0, 0)), tokens]
        + [pl.BlockSpec(memory_space=pl.ANY) for _ in into],
        out_specs=pl.BlockSpec((3, 2 * rows, LANES), lambda pair: (0, 0, pair + base)),
        out_shape=jax.ShapeDtypeStruct(qkv.shape, BF),
        scratch_shapes=[
            pltpu.VMEM((2 * rows, LANES), F32),
            pltpu.VMEM((2 * rows, LANES), F32),
        ],
        input_output_aliases={7 + i: i for i in range(len(into))},
        compiler_params=pltpu.CompilerParams(vmem_limit_bytes=VMEM),
        name="attend_backward",
    )(lo, qkv, qkv, qkv, context, lse, dcontext, *into)


def nn_pieces(x_ref, pieces):
    quarter = pieces[0].shape[0]
    weight = jnp.concatenate([piece[...] for piece in pieces], axis=0)
    return nn(x_ref[:, : 4 * quarter], weight)


def nt_pieces(grad, pieces):
    weight = jnp.concatenate([piece[...] for piece in pieces], axis=0)
    return nt(grad, weight)


def project_body(x_ref, *refs):
    pieces, shift_ref, out_ref = refs[:4], refs[4], refs[5]
    out_ref[...] = (nn_pieces(x_ref, pieces) + shift_ref[...]).astype(BF)


def project(x, pieces, shifts, kind=0):
    rows, width = x.shape
    quarter, cols = pieces[0].shape[1:]
    tile = min(cols, 512)

    kinds = shifts.shape[0]

    def part(height, first=0):
        return pl.BlockSpec((None, height, tile), lambda c, j: (c + first, 0, j))

    return pl.pallas_call(
        project_body,
        grid=(kinds, cols // tile),
        in_specs=[
            pl.BlockSpec((rows, width), lambda c, j: (0, 0)),
            *[part(quarter, kind)] * 4,
            part(1),
        ],
        out_specs=part(rows),
        out_shape=jax.ShapeDtypeStruct((kinds, rows, cols), BF),
        compiler_params=pltpu.CompilerParams(vmem_limit_bytes=VMEM),
        name="project",
    )(x, *pieces, shifts)


def project_back_body(grad_ref, *refs):
    pieces, (own_ref, send_ref, acc_ref) = refs[:4], refs[4:]
    kind = pl.program_id(0)
    rows = own_ref.shape[0]
    part = nt_pieces(grad_ref[...], pieces)

    @pl.when(kind == 0)
    def _():
        acc_ref[...] = part

    @pl.when(kind > 0)
    def _():
        acc_ref[...] += part

    @pl.when(kind == pl.num_programs(0) - 1)
    def _():
        send_ref[...] = acc_ref[:rows, :].astype(BF)
        own_ref[...] = acc_ref[rows:, :]


def project_back(grads, pieces):
    _, both, cols = grads.shape
    quarter = pieces[0].shape[1]
    rows = both // 2

    def part(height):
        return pl.BlockSpec((None, height, cols), lambda c: (c, 0, 0))

    whole = pl.BlockSpec((rows, 4 * quarter), lambda c: (0, 0))
    return pl.pallas_call(
        project_back_body,
        grid=(3,),
        in_specs=[part(both)] + [part(quarter)] * 4,
        out_specs=[whole, whole],
        out_shape=[
            jax.ShapeDtypeStruct((rows, 4 * quarter), F32),
            jax.ShapeDtypeStruct((rows, 4 * quarter), BF),
        ],
        scratch_shapes=[pltpu.VMEM((both, 4 * quarter), F32)],
        compiler_params=pltpu.CompilerParams(vmem_limit_bytes=VMEM),
        name="project_back",
    )(grads, *pieces)


HIDDEN_TILE = 512
GELU_C = 0.7978845608028654
GELU_A = 0.044715


def up_body(x_ref, *refs):
    pieces, (shift_ref, hidden_ref, slope_ref) = refs[:4], refs[4:]
    v = nn_pieces(x_ref, pieces) + shift_ref[...]
    square = v * v
    t = jnp.tanh(GELU_C * v * (1.0 + GELU_A * square))
    gate = 0.5 * (1.0 + t)
    hidden_ref[...] = (v * gate).astype(BF)
    slope = gate + (0.5 * GELU_C) * v * (1.0 - t * t) * (1.0 + (3.0 * GELU_A) * square)
    slope_ref[...] = slope.astype(BF)


def down_body(x_ref, *refs):
    pieces, slope_ref, up_pieces = refs[:4], refs[4], refs[5:9]
    dpre_ref, sum_ref, dsecond_ref = refs[9:]
    v = nn_pieces(x_ref, pieces)
    dpre = (v * slope_ref[...].astype(F32)).astype(BF)
    dpre_ref[...] = dpre
    sum_ref[...] = jnp.sum(dpre.astype(F32), axis=0, keepdims=True)
    part = nt_pieces(dpre, up_pieces)

    @pl.when(pl.program_id(0) == 0)
    def _():
        dsecond_ref[...] = part

    @pl.when(pl.program_id(0) > 0)
    def _():
        dsecond_ref[...] += part


def hidden_tile(height):
    return pl.BlockSpec((height, HIDDEN_TILE), lambda j: (0, j))


def piece_tiles(pieces):
    return [
        pl.BlockSpec((None, piece.shape[1], HIDDEN_TILE), lambda j: (0, 0, j)) for piece in pieces
    ]


def mlp_up(x, pieces, shift):
    rows, width = x.shape
    hidden = shift.shape[1]
    return pl.pallas_call(
        up_body,
        grid=(hidden // HIDDEN_TILE,),
        in_specs=[pl.BlockSpec((rows, width), lambda j: (0, 0))]
        + piece_tiles(pieces)
        + [hidden_tile(1)],
        out_specs=[hidden_tile(rows), hidden_tile(rows)],
        out_shape=[jax.ShapeDtypeStruct((rows, hidden), BF)] * 2,
        compiler_params=pltpu.CompilerParams(vmem_limit_bytes=VMEM),
        name="mlp_up",
    )(x, *pieces, shift)


def mlp_down(x, pieces, slope, up_pieces):
    rows, width = x.shape
    hidden = slope.shape[1]
    whole = pl.BlockSpec((rows, width), lambda j: (0, 0))
    return pl.pallas_call(
        down_body,
        grid=(hidden // HIDDEN_TILE,),
        in_specs=[whole] + piece_tiles(pieces) + [hidden_tile(rows)] + piece_tiles(up_pieces),
        out_specs=[hidden_tile(rows), hidden_tile(1), whole],
        out_shape=[
            jax.ShapeDtypeStruct((rows, hidden), BF),
            jax.ShapeDtypeStruct((1, hidden), F32),
            jax.ShapeDtypeStruct((rows, width), F32),
        ],
        compiler_params=pltpu.CompilerParams(vmem_limit_bytes=VMEM),
        name="mlp_down",
    )(x, *pieces, slope, *up_pieces)


def grad_body(x_ref, y_ref, *refs):
    pieces, turned = refs[-5:-1], refs[-1]
    first = (pl.program_id(0) == 0) & (pl.program_id(1) == 0)

    @pl.when(first)
    def _():
        turned[...] = x_ref[...].T

    quarter = pieces[0].shape[0]
    y = y_ref[...]
    for i, piece in enumerate(pieces):
        piece[...] = nn(turned[i * quarter : (i + 1) * quarter, :], y).astype(BF)


def weight_grads(x, y, kinds=1, place=0, into=()):
    rows, width = x.shape
    count, _, cols = y.shape
    tile = 512
    piece = jax.ShapeDtypeStruct((kinds, width // 4, cols), BF)
    return pl.pallas_call(
        grad_body,
        grid=(count, cols // tile),
        in_specs=[
            pl.BlockSpec((rows, width), lambda c, j: (0, 0)),
            pl.BlockSpec((None, rows, tile), lambda c, j: (c, 0, j)),
        ]
        + [pl.BlockSpec(memory_space=pl.ANY) for _ in into],
        out_specs=[pl.BlockSpec((None, width // 4, tile), lambda c, j: (c + place, 0, j))] * 4,
        out_shape=[piece] * 4,
        scratch_shapes=[pltpu.VMEM((width, rows), BF)],
        input_output_aliases={2 + i: i for i in range(len(into))},
        compiler_params=pltpu.CompilerParams(vmem_limit_bytes=VMEM),
        name="weight_grads",
    )(x, y, *into)


def out_body(table, x_ref, *refs):
    pieces, (middle_ref, shift_ref, out_ref, acc_ref) = refs[:4], refs[4:]
    step = pl.program_id(0)
    part = nt_pieces(x_ref[...], pieces)

    @pl.when(step == 0)
    def _():
        acc_ref[...] = part + middle_ref[...] + shift_ref[...]

    @pl.when(step > 0)
    def _():
        acc_ref[...] += part

    @pl.when(step == pl.num_programs(0) - 1)
    def _():
        lanes = out_ref.shape[1] // table.shape[0]
        for j in range(table.shape[0]):
            moved = pl.ds(pl.multiple_of(table[j] * lanes, lanes), lanes)
            out_ref[:, moved] = acc_ref[:, j * lanes : (j + 1) * lanes]


def mlp_out(hidden, pieces, middle, shift, blocks):
    rows, width = middle.shape
    moves = (width // blocks.shape[0]) % 128 == 0
    table = blocks if moves else jnp.zeros((1,), jnp.int32)
    whole = pl.BlockSpec((rows, width), lambda j: (0, 0))
    out = pl.pallas_call(
        out_body,
        grid=(hidden.shape[1] // HIDDEN_TILE,),
        in_specs=[pl.BlockSpec(memory_space=pltpu.SMEM), hidden_tile(rows)]
        + piece_tiles(pieces)
        + [whole, pl.BlockSpec((1, width), lambda j: (0, 0))],
        out_specs=whole,
        out_shape=jax.ShapeDtypeStruct((rows, width), F32),
        scratch_shapes=[pltpu.VMEM((rows, width), F32)],
        compiler_params=pltpu.CompilerParams(vmem_limit_bytes=VMEM),
        name="mlp_out",
    )(table, hidden, *pieces, middle, shift)
    return out if moves else reorder(out, blocks, back=True)


def normalize_body(before_ref, own_ref, gain_ref, shift_ref, out_ref):
    for part, ref in enumerate((before_ref, own_ref)):
        values = layer_norm(ref[...].astype(F32), gain_ref[...], shift_ref[...])
        out_ref[part] = values.astype(BF)


def normalize_both(before, own, gain, shift):
    rows, width = own.shape
    tile = pl.BlockSpec((rows // 4, width), lambda i: (i, 0))
    vector = pl.BlockSpec((1, width), lambda i: (0, 0))
    out = pl.pallas_call(
        normalize_body,
        grid=(4,),
        in_specs=[tile, tile, vector, vector],
        out_specs=pl.BlockSpec((2, rows // 4, width), lambda i: (0, i, 0)),
        out_shape=jax.ShapeDtypeStruct((2, rows, width), BF),
        name="normalize",
    )(before, own, gain, shift)
    return out.reshape(2 * rows, width)


def lowest_keys(lengths, rows):
    count = lengths.shape[0]
    step = jnp.arange(count, dtype=jnp.int32)
    ends = jnp.sum(jnp.where(step[None, :] <= step[:, None], lengths[None, :], 0), axis=1)
    base = lax.axis_index("tp") * rows
    places = base + jnp.arange(rows, dtype=jnp.int32)
    begins = jnp.max(jnp.where(ends[:, None] <= places[None, :], ends[:, None], 0), axis=0)
    return (begins - base + rows).astype(jnp.int32)[None, :]


def per_device(
    inputs,
    seq_lengths,
    qkv_w,
    out_w,
    fc_w,
    proj_w,
    ln1_gain,
    ln1_bias,
    q_bias,
    v_bias,
    out_bias,
    ln2_gain,
    ln2_bias,
    fc_bias,
    proj_bias,
    cotangent,
):
    rows = inputs.shape[0]
    quarter = inputs.shape[1] // 4
    tp_size = lax.axis_size("tp")
    masks = step_masks()
    near, far = masks[:-1], masks[-1:]
    blocks = slot_blocks()
    exchanged = [True, True, False, False, True, True, True, False, True]
    shards = [v.shape[0] for v in (ln1_gain, ln1_bias, q_bias, v_bias, out_bias)]
    shards += [v.shape[0] for v in (ln2_gain, ln2_bias, fc_bias, proj_bias)]
    bits = list(range(lax.axis_size("fsdp").bit_length() - 1))[::-1]

    def dot_nt(left, right):
        return jnp.einsum("rj,ij->ri", left, right, preferred_element_type=F32)

    def wide_nt(left, pieces, kind=0):
        return jnp.concatenate([dot_nt(left, piece[kind]) for piece in pieces], axis=1)

    def dot_pieces(left, pieces, kind):
        return sum(
            jnp.dot(quarter_of(left, i), piece[kind], preferred_element_type=F32)
            for i, piece in enumerate(pieces)
        )

    def quarter_of(values, i):
        return values[:, i * quarter : (i + 1) * quarter]

    attn_part = jnp.concatenate([qkv_w, out_w.T[None]], axis=0)
    attn_got = rotations(attn_part)
    pack = gather_vectors_fsdp(
        [ln1_gain, ln1_bias, q_bias, v_bias, out_bias, ln2_gain, ln2_bias, fc_bias, proj_bias]
    )
    own = reorder(inputs, blocks)
    cot = reorder(cotangent, blocks)
    lo = lowest_keys(seq_lengths[0], rows)
    proj_part = proj_w.T[None]

    attn_got, pack, own, cot, fc_part, proj_part = join(
        attn_got, pack, own, cot, fc_w[None], proj_part
    )
    attn_held, attn_got = gather_raw(assemble_tp(attn_part, attn_got), near)
    pack_got = rotations(pack)

    attn_got, pack_got, own = join(attn_got, pack_got, own)
    before = lax.ppermute(own, "tp", [(i, i + 1) for i in range(tp_size - 1)])
    attn_a, attn_b = gather_raw(grow(attn_held, attn_got), far)
    attn_c = core_swap(attn_a)
    (
        gain_one,
        shift_one,
        query_shift,
        value_shift,
        attn_shift,
        gain_two,
        shift_two,
        hidden_shift,
        mlp_shift,
    ) = spread_vectors(pack, pack_got, shards, exchanged, blocks)

    attn_b, attn_c, before, gain_one, fc_part = join(attn_b, attn_c, before, gain_one, fc_part)
    attn_d = core_swap(attn_b)
    fc_got = rotations(fc_part)
    first_both = normalize_both(before, own, gain_one, shift_one)

    attn_d, first_both = join(attn_d, first_both)
    attn = (attn_a, attn_b, attn_c, attn_d)
    shifts = jnp.stack([query_shift, jnp.zeros_like(query_shift), value_shift])
    qkv = project(first_both, attn, shifts)

    fc_got, qkv = join(fc_got, qkv)
    fc_held, fc_step = gather_raw(assemble_tp(fc_part, fc_got), near)
    context, lse = attention_forward(lo, qkv, 0, 2)

    fc_step, context, lse, proj_part = join(fc_step, context, lse, proj_part)
    fc_a, fc_b = gather_raw(grow(fc_held, fc_step), far)
    fc_c = core_swap(fc_a)
    proj_got = rotations(proj_part)
    context, lse = attention_forward(lo, qkv, 1, 2, (context, lse))
    residual = own.astype(F32)
    middle = residual + wide_nt(context, attn, 3) + attn_shift
    second_f, pull_two = jax.vjp(layer_norm, middle, gain_two[0], shift_two[0])
    second = second_f.astype(BF)

    fc_b, fc_c, proj_got, second = join(fc_b, fc_c, proj_got, second)
    fc_d = core_swap(fc_b)
    proj_slab = assemble_tp(proj_part, proj_got)

    fc_d, proj_slab, second = join(fc_d, proj_slab, second)
    fc = (fc_a, fc_b, fc_c, fc_d)
    proj_held, proj_step = gather_raw(proj_slab, near)
    hidden, slope = mlp_up(second, fc, hidden_shift)

    proj_step, hidden, slope = join(proj_step, hidden, slope)
    proj_a, proj_b = gather_raw(grow(proj_held, proj_step), far)
    proj_c = core_swap(proj_a)
    dproj = weight_grads(cot, hidden[None])
    dproj_got = [core_swap(dproj[3]), core_swap(dproj[2])]

    proj_b, proj_c, dproj_got, dproj = join(proj_b, proj_c, dproj_got, dproj)
    proj_d = core_swap(proj_b)
    dproj_send = add_low(dproj[1], dproj_got[0])

    proj_d, dproj_send, second = join(proj_d, dproj_send, second)
    proj = (proj_a, proj_b, proj_c, proj_d)
    _, dproj_got[0] = scatter_raw(dproj[0], dproj_send, far)
    dpre, dhidden_bias, dsecond = mlp_down(cot, proj, slope, fc)
    dfc = weight_grads(second, dpre[None])

    *dproj_got, dfc, dsecond = join(*dproj_got, dfc, dsecond)
    dfc_got = [core_swap(dfc[3]), core_swap(dfc[2])]
    dproj_keep = add_low(dproj[0], dproj_got[1])
    dproj_keep, dproj_got = scatter_raw(*split_add(dproj_keep, dproj_got[0]), near[::-1])
    dmiddle_norm, dgain_two, dshift_two = pull_two(dsecond)
    dmiddle = cot.astype(F32) + dmiddle_norm
    dattn = dmiddle.astype(BF)
    dcontext = project(dattn, attn, jnp.zeros((1, 1, context.shape[1]), F32), 3)[0]
    dout = weight_grads(dattn, context[None], kinds=4, place=3)

    dproj_got, dcontext, dout, dfc_got = join(dproj_got, dcontext, dout, dfc_got)
    _, dfc_got[0] = scatter_raw(dfc[0], add_low(dfc[1], dfc_got[0]), far)
    dproj_parts = scatter_tp_raw(add_low(dproj_keep, dproj_got))
    dqkv = attention_backward(lo, qkv, context, lse, dcontext)

    dfc_got, dproj_parts, dqkv = join(dfc_got, dproj_parts, dqkv)
    dfc_keep = add_low(dfc[0], dfc_got[1])
    dfc_keep, dfc_got = scatter_raw(*split_add(dfc_keep, dfc_got[0]), near[::-1])

    dattn_w = weight_grads(first_both, dqkv, kinds=4, into=tuple(dout))

    dfc_got, dattn_w, dqkv = join(dfc_got, dattn_w, dqkv)
    dattn_got = [core_swap(dattn_w[3]), core_swap(dattn_w[2])]
    dfc_parts = scatter_tp_raw(add_low(dfc_keep, dfc_got))
    dfirst_own, dfirst_send = project_back(dqkv, attn)

    dattn_got, dattn_w, dfirst_own, dfirst_send, hidden, dfc_parts = join(
        dattn_got, dattn_w, dfirst_own, dfirst_send, hidden, dfc_parts
    )
    _, dattn_got[0] = scatter_raw(dattn_w[0], add_low(dattn_w[1], dattn_got[0]), far)
    dfirst_after = lax.ppermute(dfirst_send, "tp", [(i + 1, i) for i in range(tp_size - 1)])
    outputs = mlp_out(hidden, proj, middle, mlp_shift, blocks)

    dattn_got, dfirst_after, outputs, dfirst_own = join(
        dattn_got, dfirst_after, outputs, dfirst_own
    )
    dattn_keep = add_low(dattn_w[0], dattn_got[1])
    dattn_keep, dattn_got = scatter_raw(*split_add(dattn_keep, dattn_got[0]), near[::-1])
    _, pull_one = jax.vjp(layer_norm, residual, gain_one[0], shift_one[0])
    dresidual, gain_own, shift_own = pull_one(dfirst_own + dfirst_after.astype(F32))
    vectors = pack_vectors(
        [
            gain_own,
            shift_own,
            jnp.sum(dqkv[0], axis=0, dtype=F32),
            jnp.sum(dqkv[2], axis=0, dtype=F32),
            jnp.sum(dattn, axis=0, dtype=F32),
            dgain_two,
            dshift_two,
            dhidden_bias[0],
            jnp.sum(cot, axis=0, dtype=F32),
        ],
        exchanged,
        blocks,
    )

    vectors = scatter_pack(vectors, bits)

    dinputs = reorder(dmiddle + dresidual, blocks, back=True)
    fc_grad = total_tp(dfc_parts)[0]
    proj_grad = total_tp(dproj_parts)[0].T

    dattn_got, vectors, dinputs, fc_grad, proj_grad = join(
        dattn_got, vectors, dinputs, fc_grad, proj_grad
    )
    attn_parts = scatter_tp_raw(add_low(dattn_keep, dattn_got))
    vector_grads = unpack_vectors(vectors, shards, exchanged)
    attn_grad = total_tp(attn_parts)
    return (
        outputs,
        dinputs,
        attn_grad[:3],
        attn_grad[3].T,
        fc_grad,
        proj_grad,
        *vector_grads,
    )


def solution(mesh):
    vector = P(("fsdp", "tp"))
    tokens = P(("fsdp", "tp"), None)
    weights = (P(None, "fsdp", "tp"), P("tp", "fsdp"), P("fsdp", "tp"), P("tp", "fsdp"))
    return jax.shard_map(
        per_device,
        mesh=mesh,
        in_specs=(tokens, P("fsdp", None), *weights, *([vector] * 9), tokens),
        out_specs=(tokens, tokens, *weights, *([vector] * 9)),
        check_vma=False,
    )
```

```python
import jax
import jax.numpy as jnp
from jax import lax
import numpy as np
from jax.experimental import pallas as pl
from jax.experimental.pallas import tpu as pltpu
from jax.sharding import PartitionSpec as P

HD = 64
QT = 256
EPSILON = 1e-05
MASKED = -1e30
VMEM = 40 * 2**20
BF = jnp.bfloat16
F32 = jnp.float32


def layer_norm(values, gain, shift):
    center = jnp.mean(values, axis=-1, keepdims=True)
    offset = values - center
    spread = jnp.mean(offset * offset, axis=-1, keepdims=True)
    return offset * lax.rsqrt(spread + EPSILON) * gain + shift


def gelu(values):
    return jax.nn.gelu(values, approximate=True)


def exchange(item, axis, mask):
    size = lax.axis_size(axis)
    return lax.ppermute(item, axis, [(i, i ^ mask) for i in range(size)])


def exchange_by_core(item, even_mask, odd_mask):
    size = lax.axis_size("fsdp")
    pairs = [(i, i ^ (odd_mask if i % 2 else even_mask)) for i in range(size)]
    return lax.ppermute(item, "fsdp", pairs)


def rotate(item, step):
    size = lax.axis_size("tp")
    return lax.ppermute(item, "tp", [(i, (i + step) % size) for i in range(size)])


def step_masks():
    bits = [1 << b for b in range(1, lax.axis_size("fsdp").bit_length() - 1)]
    return list(zip(bits, bits[::-1]))


def slot_blocks():
    held = [(0, 0)]
    for even, odd in step_masks():
        held = held + [(a ^ even, b ^ odd) for a, b in held]
    held = held + [(b ^ 1, a ^ 1) for a, b in held]
    table = np.asarray(held, np.int32)
    mine = lax.axis_index("fsdp")
    return mine ^ jnp.where(mine % 2 == 0, table[:, 0], table[:, 1])


def rotations(part):
    return [rotate(part, k) for k in range(1, lax.axis_size("tp"))]


def assemble_tp(part, got):
    size = lax.axis_size("tp")
    mine = lax.axis_index("tp")
    return jnp.concatenate(
        [lax.select_n((mine - p) % size, part, *got) for p in range(size)], axis=-1
    )


def grow(held, got):
    return jnp.concatenate([held, got], axis=1)


def gather_raw(held, masks):
    for even, odd in masks[:-1]:
        held = grow(held, exchange_by_core(held, even, odd))
    held = lax.optimization_barrier(held)
    return held, exchange_by_core(held, *masks[-1])


def add_low(left, right):
    return (left.astype(F32) + right.astype(F32)).astype(BF)


def split_add(left, right):
    half = left.shape[1] // 2
    return (
        add_low(left[:, :half], right[:, :half]),
        add_low(left[:, half:], right[:, half:]),
    )


def scatter_raw(keep, send, masks):
    for even, odd in masks[:-1]:
        keep, send = split_add(keep, exchange_by_core(send, even, odd))
    return keep, exchange_by_core(send, *masks[-1])


def core_swap(item):
    return exchange(item, "fsdp", 1)


def scatter_tp_raw(slab):
    size = lax.axis_size("tp")
    mine = lax.axis_index("tp")
    cols = slab.shape[-1] // size
    parts = [slab[:, :, p * cols : (p + 1) * cols] for p in range(size)]
    got = [rotate(lax.select_n((mine + k) % size, *parts), k) for k in range(1, size)]
    return [lax.select_n(mine, *parts), *got]


def total_tp(parts):
    total = parts[0].astype(F32)
    for part in parts[1:]:
        total = total + part.astype(F32)
    return total


def join(*items):
    return jax.tree.unflatten(
        jax.tree.structure(items), lax.optimization_barrier(tuple(jax.tree.leaves(items)))
    )


def pick(items, order):
    slot = jnp.arange(items.shape[0], dtype=jnp.int32)
    chosen = (order[:, None] == slot[None, :]).reshape(
        (items.shape[0],) * 2 + (1,) * (items.ndim - 1)
    )
    return jnp.sum(jnp.where(chosen, items[None], jnp.zeros_like(items)[None]), axis=1).astype(
        items.dtype
    )


def inverse(blocks):
    slot = jnp.arange(blocks.shape[0], dtype=jnp.int32)
    return jnp.sum(jnp.where(blocks[None, :] == slot[:, None], slot[None, :], 0), axis=1)


def reorder(values, blocks, back=False):
    rows, width = values.shape
    count = blocks.shape[0]
    lanes = width // count
    if lanes % 128:
        order = inverse(blocks) if back else blocks
        split = pick(values.reshape(rows, count, lanes).swapaxes(0, 1), order)
        return split.swapaxes(0, 1).reshape(rows, width)

    def body(table, source, target):
        for j in range(count):
            moved = pl.ds(pl.multiple_of(table[j] * lanes, lanes), lanes)
            plain = pl.ds(j * lanes, lanes)
            if back:
                target[:, moved] = source[:, plain]
            else:
                target[:, plain] = source[:, moved]

    tile = pl.BlockSpec((rows // 4, width), lambda i: (i, 0))
    return pl.pallas_call(
        body,
        grid=(4,),
        in_specs=[pl.BlockSpec(memory_space=pltpu.SMEM), tile],
        out_specs=tile,
        out_shape=jax.ShapeDtypeStruct(values.shape, values.dtype),
        name="reorder",
    )(blocks, values)


def gather_vectors_fsdp(vectors):
    width = vectors[0].shape[0]
    pack = jnp.concatenate([v.reshape(1, 1, -1, width) for v in vectors], axis=2)
    where = lax.axis_index("fsdp")
    for b in range(lax.axis_size("fsdp").bit_length() - 1):
        other = exchange(pack, "fsdp", 1 << b)
        high = (where >> b) % 2 == 1
        pack = jnp.concatenate(
            [jnp.where(high, other, pack), jnp.where(high, pack, other)], axis=0
        )
    return pack


def spread_vectors(pack, got, lengths, which, blocks):
    size = lax.axis_size("tp")
    mine = lax.axis_index("tp")
    width = pack.shape[3]
    pack = jnp.concatenate(
        [lax.select_n((mine - p) % size, pack, *got) for p in range(size)], axis=1
    )
    moved = pick(pack, blocks)
    out, at = [], 0
    for length, exchanged in zip(lengths, which):
        source = moved if exchanged else pack
        count = length // width
        out.append(source[:, :, at : at + count].reshape(1, -1).astype(F32))
        at += count
    return out


def pack_vectors(vectors):
    count = lax.axis_size("fsdp")
    size = lax.axis_size("tp")
    return jnp.concatenate([v.reshape(count, size, -1) for v in vectors], axis=2)


def scatter_pack(pack, bits):
    where = lax.axis_index("fsdp")
    for b in bits:
        half = pack.shape[0] // 2
        high = (where >> b) % 2 == 1
        low_part, high_part = pack[:half], pack[half:]
        keep = jnp.where(high, high_part, low_part)
        send = jnp.where(high, low_part, high_part)
        pack = keep + exchange(send, "fsdp", 1 << b)
    return pack


def unpack_vectors(pack, lengths):
    mine = lax.axis_index("tp")
    size = lax.axis_size("tp")
    rows = [pack[0, p] for p in range(size)]
    total = lax.select_n(mine, *rows)
    for k in range(1, size):
        total = total + rotate(lax.select_n((mine + k) % size, *rows), k)
    ends = np.cumsum(lengths)
    return [total[end - length : end] for end, length in zip(ends, lengths)]


def head_lanes(shape, head):
    lane = lax.broadcasted_iota(jnp.int32, shape, 1)
    return (lane >= head * HD) & (lane < (head + 1) * HD)


def nt(left, right):
    return lax.dot_general(left, right, (((1,), (1,)), ((), ())), preferred_element_type=F32)


def nn(left, right):
    return lax.dot_general(left, right, (((1,), (0,)), ((), ())), preferred_element_type=F32)


def allowed_keys(lo_row, start, keys, queries, rows):
    key = start + lax.broadcasted_iota(jnp.int32, (keys, queries), 0)
    query = rows + start + lax.broadcasted_iota(jnp.int32, (keys, queries), 1)
    return (key >= lo_row) & (key <= query)


def attend_forward(lo_ref, q_ref, k_ref, v_ref, *refs):
    ctx_ref, lse_ref = refs[-2:]
    rows = q_ref.shape[0]
    width = rows + QT
    value_t = v_ref[...].T
    for tile in range(rows // QT):
        start = tile * QT
        query = q_ref[pl.ds(start, QT), :] * jnp.asarray(HD**-0.5, BF)
        keys = k_ref[pl.ds(start, width), :]
        allowed = allowed_keys(lo_ref[:, start : start + QT], start, width, QT, rows)
        parts = []
        for head in range(2):
            query_h = jnp.where(head_lanes(query.shape, head), query, jnp.zeros_like(query))
            scores = jnp.where(allowed, nt(keys, query_h), MASKED)
            peak = jnp.max(scores, axis=0, keepdims=True)
            expo = jnp.exp(scores - peak)
            total = jnp.sum(expo, axis=0, keepdims=True)
            attend = expo.astype(BF)
            parts.append(
                nn(value_t[head * HD : (head + 1) * HD, start : start + width], attend)
                * (1.0 / total)
            )
            lse_ref[0, head : head + 1, start : start + QT] = peak + jnp.log(total)
        ctx_ref[pl.ds(start, QT), :] = jnp.concatenate(parts, axis=0).T.astype(BF)


def attend_backward(lo_ref, q_ref, k_ref, v_ref, ctx_ref, lse_ref, grad_ref, *refs):
    out_ref, dk_acc, dv_acc = refs[-3:]
    rows = q_ref.shape[0]
    width = rows + QT
    scale = HD**-0.5
    dk_acc[...] = jnp.zeros_like(dk_acc)
    dv_acc[...] = jnp.zeros_like(dv_acc)
    key_t = k_ref[...].T
    for tile in range(rows // QT):
        start = tile * QT
        query = q_ref[pl.ds(start, QT), :] * jnp.asarray(scale, BF)
        grad = grad_ref[pl.ds(start, QT), :]
        keys = k_ref[pl.ds(start, width), :]
        values = v_ref[pl.ds(start, width), :]
        allowed = allowed_keys(lo_ref[:, start : start + QT], start, width, QT, rows)
        inner_t = (grad.astype(F32) * ctx_ref[pl.ds(start, QT), :].astype(F32)).T
        parts = []
        dk_sum, dv_sum = None, None
        for head in range(2):
            lanes = head_lanes(query.shape, head)
            query_h = jnp.where(lanes, query, jnp.zeros_like(query))
            grad_h = jnp.where(lanes, grad, jnp.zeros_like(grad))
            scores = jnp.where(allowed, nt(keys, query_h), MASKED)
            attend = jnp.exp(scores - lse_ref[0, head : head + 1, start : start + QT])
            inner = jnp.sum(inner_t[head * HD : (head + 1) * HD, :], axis=0, keepdims=True)
            dscores = (attend * (nt(values, grad_h) - inner)).astype(BF)
            dv_part = nn(attend.astype(BF), grad_h)
            dk_part = nn(dscores, query_h)
            dv_sum = dv_part if dv_sum is None else dv_sum + dv_part
            dk_sum = dk_part if dk_sum is None else dk_sum + dk_part
            parts.append(
                nn(key_t[head * HD : (head + 1) * HD, start : start + width], dscores) * scale
            )
        out_ref[0, pl.ds(rows + start, QT), :] = jnp.concatenate(parts, axis=0).T.astype(BF)
        dk_acc[pl.ds(start, width), :] += dk_sum
        dv_acc[pl.ds(start, width), :] += dv_sum
    out_ref[0, pl.ds(0, rows), :] = jnp.zeros((rows, out_ref.shape[2]), BF)
    out_ref[1] = dk_acc[...].astype(BF)
    out_ref[2] = dv_acc[...].astype(BF)


LANES = 2 * HD


def attention_specs(rows, base):
    def projected(kind, height, block):
        return pl.BlockSpec((None, height, LANES), lambda pair: (kind, block, pair + base))

    return [
        pl.BlockSpec((1, rows), lambda pair: (0, 0)),
        projected(0, rows, 1),
        projected(1, 2 * rows, 0),
        projected(2, 2 * rows, 0),
    ]


def attention_forward(lo, qkv, part=0, parts=1, into=()):
    rows, width = qkv.shape[1] // 2, qkv.shape[2]
    pairs = width // LANES // parts
    base = pairs * part
    return pl.pallas_call(
        attend_forward,
        grid=(pairs,),
        in_specs=attention_specs(rows, base)
        + [pl.BlockSpec(memory_space=pl.ANY) for _ in into],
        out_specs=[
            pl.BlockSpec((rows, LANES), lambda pair: (0, pair + base)),
            pl.BlockSpec((1, 2, rows), lambda pair: (pair + base, 0, 0)),
        ],
        out_shape=[
            jax.ShapeDtypeStruct((rows, width), BF),
            jax.ShapeDtypeStruct((width // LANES, 2, rows), F32),
        ],
        input_output_aliases={4 + i: i for i in range(len(into))},
        compiler_params=pltpu.CompilerParams(vmem_limit_bytes=VMEM),
        name="attend_forward",
    )(lo, qkv, qkv, qkv, *into)


def attention_backward(lo, qkv, context, lse, dcontext, part=0, parts=1, into=()):
    rows, width = qkv.shape[1] // 2, qkv.shape[2]
    pairs = width // LANES // parts
    base = pairs * part
    tokens = pl.BlockSpec((rows, LANES), lambda pair: (0, pair + base))
    return pl.pallas_call(
        attend_backward,
        grid=(pairs,),
        in_specs=attention_specs(rows, base)
        + [tokens, pl.BlockSpec((1, 2, rows), lambda pair: (pair + base, 0, 0)), tokens]
        + [pl.BlockSpec(memory_space=pl.ANY) for _ in into],
        out_specs=pl.BlockSpec((3, 2 * rows, LANES), lambda pair: (0, 0, pair + base)),
        out_shape=jax.ShapeDtypeStruct(qkv.shape, BF),
        scratch_shapes=[
            pltpu.VMEM((2 * rows, LANES), F32),
            pltpu.VMEM((2 * rows, LANES), F32),
        ],
        input_output_aliases={7 + i: i for i in range(len(into))},
        compiler_params=pltpu.CompilerParams(vmem_limit_bytes=VMEM),
        name="attend_backward",
    )(lo, qkv, qkv, qkv, context, lse, dcontext, *into)


def nn_pieces(x_ref, pieces):
    quarter = pieces[0].shape[0]
    weight = jnp.concatenate([piece[...] for piece in pieces], axis=0)
    return nn(x_ref[:, : 4 * quarter], weight)


def nt_pieces(grad, pieces):
    weight = jnp.concatenate([piece[...] for piece in pieces], axis=0)
    return nt(grad, weight)


def project_body(x_ref, *refs):
    pieces, shift_ref, out_ref = refs[:4], refs[4], refs[5]
    out_ref[...] = (nn_pieces(x_ref, pieces) + shift_ref[...]).astype(BF)


def project(x, pieces, shifts, kind=0):
    rows, width = x.shape
    quarter, cols = pieces[0].shape[1:]
    tile = min(cols, 512)

    kinds = shifts.shape[0]

    def part(height, first=0):
        return pl.BlockSpec((None, height, tile), lambda c, j: (c + first, 0, j))

    return pl.pallas_call(
        project_body,
        grid=(kinds, cols // tile),
        in_specs=[
            pl.BlockSpec((rows, width), lambda c, j: (0, 0)),
            *[part(quarter, kind)] * 4,
            part(1),
        ],
        out_specs=part(rows),
        out_shape=jax.ShapeDtypeStruct((kinds, rows, cols), BF),
        compiler_params=pltpu.CompilerParams(vmem_limit_bytes=VMEM),
        name="project",
    )(x, *pieces, shifts)


def project_back_body(grad_ref, *refs):
    pieces, (own_ref, send_ref, acc_ref) = refs[:4], refs[4:]
    kind = pl.program_id(0)
    rows = own_ref.shape[0]
    part = nt_pieces(grad_ref[...], pieces)

    @pl.when(kind == 0)
    def _():
        acc_ref[...] = part

    @pl.when(kind > 0)
    def _():
        acc_ref[...] += part

    @pl.when(kind == pl.num_programs(0) - 1)
    def _():
        send_ref[...] = acc_ref[:rows, :].astype(BF)
        own_ref[...] = acc_ref[rows:, :]


def project_back(grads, pieces):
    _, both, cols = grads.shape
    quarter = pieces[0].shape[1]
    rows = both // 2

    def part(height):
        return pl.BlockSpec((None, height, cols), lambda c: (c, 0, 0))

    whole = pl.BlockSpec((rows, 4 * quarter), lambda c: (0, 0))
    return pl.pallas_call(
        project_back_body,
        grid=(3,),
        in_specs=[part(both)] + [part(quarter)] * 4,
        out_specs=[whole, whole],
        out_shape=[
            jax.ShapeDtypeStruct((rows, 4 * quarter), F32),
            jax.ShapeDtypeStruct((rows, 4 * quarter), BF),
        ],
        scratch_shapes=[pltpu.VMEM((both, 4 * quarter), F32)],
        compiler_params=pltpu.CompilerParams(vmem_limit_bytes=VMEM),
        name="project_back",
    )(grads, *pieces)


HIDDEN_TILE = 512
GELU_C = 0.7978845608028654
GELU_A = 0.044715


def up_body(x_ref, *refs):
    pieces, (shift_ref, hidden_ref, slope_ref) = refs[:4], refs[4:]
    v = nn_pieces(x_ref, pieces) + shift_ref[...]
    square = v * v
    t = jnp.tanh(GELU_C * v * (1.0 + GELU_A * square))
    gate = 0.5 * (1.0 + t)
    hidden_ref[...] = (v * gate).astype(BF)
    slope = gate + (0.5 * GELU_C) * v * (1.0 - t * t) * (1.0 + (3.0 * GELU_A) * square)
    slope_ref[...] = slope.astype(BF)


def down_body(x_ref, *refs):
    pieces, slope_ref, up_pieces = refs[:4], refs[4], refs[5:9]
    dpre_ref, sum_ref, dsecond_ref = refs[9:]
    v = nn_pieces(x_ref, pieces)
    dpre = (v * slope_ref[...].astype(F32)).astype(BF)
    dpre_ref[...] = dpre
    sum_ref[...] = jnp.sum(dpre.astype(F32), axis=0, keepdims=True)
    part = nt_pieces(dpre, up_pieces)

    @pl.when(pl.program_id(0) == 0)
    def _():
        dsecond_ref[...] = part

    @pl.when(pl.program_id(0) > 0)
    def _():
        dsecond_ref[...] += part


def hidden_tile(height):
    return pl.BlockSpec((height, HIDDEN_TILE), lambda j: (0, j))


def piece_tiles(pieces):
    return [
        pl.BlockSpec((None, piece.shape[1], HIDDEN_TILE), lambda j: (0, 0, j)) for piece in pieces
    ]


def mlp_up(x, pieces, shift):
    rows, width = x.shape
    hidden = shift.shape[1]
    return pl.pallas_call(
        up_body,
        grid=(hidden // HIDDEN_TILE,),
        in_specs=[pl.BlockSpec((rows, width), lambda j: (0, 0))]
        + piece_tiles(pieces)
        + [hidden_tile(1)],
        out_specs=[hidden_tile(rows), hidden_tile(rows)],
        out_shape=[jax.ShapeDtypeStruct((rows, hidden), BF)] * 2,
        compiler_params=pltpu.CompilerParams(vmem_limit_bytes=VMEM),
        name="mlp_up",
    )(x, *pieces, shift)


def mlp_down(x, pieces, slope, up_pieces):
    rows, width = x.shape
    hidden = slope.shape[1]
    whole = pl.BlockSpec((rows, width), lambda j: (0, 0))
    return pl.pallas_call(
        down_body,
        grid=(hidden // HIDDEN_TILE,),
        in_specs=[whole] + piece_tiles(pieces) + [hidden_tile(rows)] + piece_tiles(up_pieces),
        out_specs=[hidden_tile(rows), hidden_tile(1), whole],
        out_shape=[
            jax.ShapeDtypeStruct((rows, hidden), BF),
            jax.ShapeDtypeStruct((1, hidden), F32),
            jax.ShapeDtypeStruct((rows, width), F32),
        ],
        compiler_params=pltpu.CompilerParams(vmem_limit_bytes=VMEM),
        name="mlp_down",
    )(x, *pieces, slope, *up_pieces)


def grad_body(x_ref, y_ref, *refs):
    pieces, turned = refs[-5:-1], refs[-1]
    first = (pl.program_id(0) == 0) & (pl.program_id(1) == 0)

    @pl.when(first)
    def _():
        turned[...] = x_ref[...].T

    quarter = pieces[0].shape[0]
    y = y_ref[...]
    for i, piece in enumerate(pieces):
        piece[...] = nn(turned[i * quarter : (i + 1) * quarter, :], y).astype(BF)


def weight_grads(x, y, kinds=1, place=0, into=()):
    rows, width = x.shape
    count, _, cols = y.shape
    tile = 512
    piece = jax.ShapeDtypeStruct((kinds, width // 4, cols), BF)
    return pl.pallas_call(
        grad_body,
        grid=(count, cols // tile),
        in_specs=[
            pl.BlockSpec((rows, width), lambda c, j: (0, 0)),
            pl.BlockSpec((None, rows, tile), lambda c, j: (c, 0, j)),
        ]
        + [pl.BlockSpec(memory_space=pl.ANY) for _ in into],
        out_specs=[pl.BlockSpec((None, width // 4, tile), lambda c, j: (c + place, 0, j))] * 4,
        out_shape=[piece] * 4,
        scratch_shapes=[pltpu.VMEM((width, rows), BF)],
        input_output_aliases={2 + i: i for i in range(len(into))},
        compiler_params=pltpu.CompilerParams(vmem_limit_bytes=VMEM),
        name="weight_grads",
    )(x, y, *into)


def out_body(table, x_ref, *refs):
    pieces, (middle_ref, shift_ref, out_ref, acc_ref) = refs[:4], refs[4:]
    step = pl.program_id(0)
    part = nt_pieces(x_ref[...], pieces)

    @pl.when(step == 0)
    def _():
        acc_ref[...] = part + middle_ref[...] + shift_ref[...]

    @pl.when(step > 0)
    def _():
        acc_ref[...] += part

    @pl.when(step == pl.num_programs(0) - 1)
    def _():
        lanes = out_ref.shape[1] // table.shape[0]
        for j in range(table.shape[0]):
            moved = pl.ds(pl.multiple_of(table[j] * lanes, lanes), lanes)
            out_ref[:, moved] = acc_ref[:, j * lanes : (j + 1) * lanes]


def mlp_out(hidden, pieces, middle, shift, blocks):
    rows, width = middle.shape
    moves = (width // blocks.shape[0]) % 128 == 0
    table = blocks if moves else jnp.zeros((1,), jnp.int32)
    whole = pl.BlockSpec((rows, width), lambda j: (0, 0))
    out = pl.pallas_call(
        out_body,
        grid=(hidden.shape[1] // HIDDEN_TILE,),
        in_specs=[pl.BlockSpec(memory_space=pltpu.SMEM), hidden_tile(rows)]
        + piece_tiles(pieces)
        + [whole, pl.BlockSpec((1, width), lambda j: (0, 0))],
        out_specs=whole,
        out_shape=jax.ShapeDtypeStruct((rows, width), F32),
        scratch_shapes=[pltpu.VMEM((rows, width), F32)],
        compiler_params=pltpu.CompilerParams(vmem_limit_bytes=VMEM),
        name="mlp_out",
    )(table, hidden, *pieces, middle, shift)
    return out if moves else reorder(out, blocks, back=True)


def normalize_body(before_ref, own_ref, gain_ref, shift_ref, out_ref):
    for part, ref in enumerate((before_ref, own_ref)):
        values = layer_norm(ref[...].astype(F32), gain_ref[...], shift_ref[...])
        out_ref[part] = values.astype(BF)


def normalize_both(before, own, gain, shift):
    rows, width = own.shape
    tile = pl.BlockSpec((rows // 4, width), lambda i: (i, 0))
    vector = pl.BlockSpec((1, width), lambda i: (0, 0))
    out = pl.pallas_call(
        normalize_body,
        grid=(4,),
        in_specs=[tile, tile, vector, vector],
        out_specs=pl.BlockSpec((2, rows // 4, width), lambda i: (0, i, 0)),
        out_shape=jax.ShapeDtypeStruct((2, rows, width), BF),
        name="normalize",
    )(before, own, gain, shift)
    return out.reshape(2 * rows, width)


def lowest_keys(lengths, rows):
    count = lengths.shape[0]
    step = jnp.arange(count, dtype=jnp.int32)
    ends = jnp.sum(jnp.where(step[None, :] <= step[:, None], lengths[None, :], 0), axis=1)
    base = lax.axis_index("tp") * rows
    places = base + jnp.arange(rows, dtype=jnp.int32)
    begins = jnp.max(jnp.where(ends[:, None] <= places[None, :], ends[:, None], 0), axis=0)
    return (begins - base + rows).astype(jnp.int32)[None, :]


def per_device(
    inputs,
    seq_lengths,
    qkv_w,
    out_w,
    fc_w,
    proj_w,
    ln1_gain,
    ln1_bias,
    q_bias,
    v_bias,
    out_bias,
    ln2_gain,
    ln2_bias,
    fc_bias,
    proj_bias,
    cotangent,
):
    rows = inputs.shape[0]
    quarter = inputs.shape[1] // 4
    tp_size = lax.axis_size("tp")
    masks = step_masks()
    near, far = masks[:-1], masks[-1:]
    blocks = slot_blocks()
    exchanged = [True, True, False, False, True, True, True, False, True]
    shards = [v.shape[0] for v in (ln1_gain, ln1_bias, q_bias, v_bias, out_bias)]
    shards += [v.shape[0] for v in (ln2_gain, ln2_bias, fc_bias, proj_bias)]
    bits = list(range(lax.axis_size("fsdp").bit_length() - 1))[::-1]

    def dot_nt(left, right):
        return jnp.einsum("rj,ij->ri", left, right, preferred_element_type=F32)

    def wide_nt(left, pieces, kind=0):
        return jnp.concatenate([dot_nt(left, piece[kind]) for piece in pieces], axis=1)

    def dot_pieces(left, pieces, kind):
        return sum(
            jnp.dot(quarter_of(left, i), piece[kind], preferred_element_type=F32)
            for i, piece in enumerate(pieces)
        )

    def quarter_of(values, i):
        return values[:, i * quarter : (i + 1) * quarter]

    attn_part = jnp.concatenate([qkv_w, out_w.T[None]], axis=0)
    attn_got = rotations(attn_part)
    pack = gather_vectors_fsdp(
        [ln1_gain, ln1_bias, q_bias, v_bias, out_bias, ln2_gain, ln2_bias, fc_bias, proj_bias]
    )
    own = reorder(inputs, blocks)
    cot = reorder(cotangent, blocks)
    lo = lowest_keys(seq_lengths[0], rows)
    proj_part = proj_w.T[None]

    attn_got, pack, own, cot, fc_part, proj_part = join(
        attn_got, pack, own, cot, fc_w[None], proj_part
    )
    attn_held, attn_got = gather_raw(assemble_tp(attn_part, attn_got), near)
    pack_got = rotations(pack)

    attn_got, pack_got, own = join(attn_got, pack_got, own)
    before = lax.ppermute(own, "tp", [(i, i + 1) for i in range(tp_size - 1)])
    attn_a, attn_b = gather_raw(grow(attn_held, attn_got), far)
    attn_c = core_swap(attn_a)
    (
        gain_one,
        shift_one,
        query_shift,
        value_shift,
        attn_shift,
        gain_two,
        shift_two,
        hidden_shift,
        mlp_shift,
    ) = spread_vectors(pack, pack_got, shards, exchanged, blocks)

    attn_b, attn_c, before, gain_one, fc_part = join(attn_b, attn_c, before, gain_one, fc_part)
    attn_d = core_swap(attn_b)
    fc_got = rotations(fc_part)
    first_both = normalize_both(before, own, gain_one, shift_one)

    attn_d, first_both = join(attn_d, first_both)
    attn = (attn_a, attn_b, attn_c, attn_d)
    shifts = jnp.stack([query_shift, jnp.zeros_like(query_shift), value_shift])
    qkv = project(first_both, attn, shifts)

    fc_got, qkv = join(fc_got, qkv)
    fc_held, fc_step = gather_raw(assemble_tp(fc_part, fc_got), near)
    context, lse = attention_forward(lo, qkv, 0, 2)

    fc_step, context, lse, proj_part = join(fc_step, context, lse, proj_part)
    fc_a, fc_b = gather_raw(grow(fc_held, fc_step), far)
    fc_c = core_swap(fc_a)
    proj_got = rotations(proj_part)
    context, lse = attention_forward(lo, qkv, 1, 2, (context, lse))
    residual = own.astype(F32)
    middle = residual + wide_nt(context, attn, 3) + attn_shift
    second_f, pull_two = jax.vjp(layer_norm, middle, gain_two[0], shift_two[0])
    second = second_f.astype(BF)

    fc_b, fc_c, proj_got, second = join(fc_b, fc_c, proj_got, second)
    fc_d = core_swap(fc_b)
    proj_slab = assemble_tp(proj_part, proj_got)

    fc_d, proj_slab, second = join(fc_d, proj_slab, second)
    fc = (fc_a, fc_b, fc_c, fc_d)
    proj_held, proj_step = gather_raw(proj_slab, near)
    hidden, slope = mlp_up(second, fc, hidden_shift)

    proj_step, hidden, slope = join(proj_step, hidden, slope)
    proj_a, proj_b = gather_raw(grow(proj_held, proj_step), far)
    proj_c = core_swap(proj_a)
    dproj = weight_grads(cot, hidden[None])
    dproj_got = [core_swap(dproj[3]), core_swap(dproj[2])]

    proj_b, proj_c, dproj_got, dproj = join(proj_b, proj_c, dproj_got, dproj)
    proj_d = core_swap(proj_b)
    dproj_send = add_low(dproj[1], dproj_got[0])

    proj_d, dproj_send, second = join(proj_d, dproj_send, second)
    proj = (proj_a, proj_b, proj_c, proj_d)
    _, dproj_got[0] = scatter_raw(dproj[0], dproj_send, far)
    dpre, dhidden_bias, dsecond = mlp_down(cot, proj, slope, fc)
    dfc = weight_grads(second, dpre[None])

    *dproj_got, dfc, dsecond = join(*dproj_got, dfc, dsecond)
    dfc_got = [core_swap(dfc[3]), core_swap(dfc[2])]
    dproj_keep = add_low(dproj[0], dproj_got[1])
    dproj_keep, dproj_got = scatter_raw(*split_add(dproj_keep, dproj_got[0]), near[::-1])
    dmiddle_norm, dgain_two, dshift_two = pull_two(dsecond)
    dmiddle = cot.astype(F32) + dmiddle_norm
    dattn = dmiddle.astype(BF)
    dcontext = project(dattn, attn, jnp.zeros((1, 1, context.shape[1]), F32), 3)[0]
    dout = weight_grads(dattn, context[None], kinds=4, place=3)

    dproj_got, dcontext, dout, dfc_got = join(dproj_got, dcontext, dout, dfc_got)
    _, dfc_got[0] = scatter_raw(dfc[0], add_low(dfc[1], dfc_got[0]), far)
    dproj_parts = scatter_tp_raw(add_low(dproj_keep, dproj_got))
    dqkv = attention_backward(lo, qkv, context, lse, dcontext)

    dfc_got, dproj_parts, dqkv = join(dfc_got, dproj_parts, dqkv)
    dfc_keep = add_low(dfc[0], dfc_got[1])
    dfc_keep, dfc_got = scatter_raw(*split_add(dfc_keep, dfc_got[0]), near[::-1])

    dattn_w = weight_grads(first_both, dqkv, kinds=4, into=tuple(dout))

    dfc_got, dattn_w, dqkv = join(dfc_got, dattn_w, dqkv)
    dattn_got = [core_swap(dattn_w[3]), core_swap(dattn_w[2])]
    dfc_parts = scatter_tp_raw(add_low(dfc_keep, dfc_got))
    dfirst_own, dfirst_send = project_back(dqkv, attn)

    dattn_got, dattn_w, dfirst_own, dfirst_send, hidden, dfc_parts = join(
        dattn_got, dattn_w, dfirst_own, dfirst_send, hidden, dfc_parts
    )
    _, dattn_got[0] = scatter_raw(dattn_w[0], add_low(dattn_w[1], dattn_got[0]), far)
    dfirst_after = lax.ppermute(dfirst_send, "tp", [(i + 1, i) for i in range(tp_size - 1)])
    outputs = mlp_out(hidden, proj, middle, mlp_shift, blocks)

    proj_grad = total_tp(dproj_parts)[0].T
    early = pack_vectors([jnp.sum(dattn, axis=0, dtype=F32), dgain_two, dshift_two])
    early = jnp.concatenate(
        [
            pick(
                jnp.concatenate([early, pack_vectors([jnp.sum(cot, axis=0, dtype=F32)])], axis=2),
                inverse(blocks),
            ),
            pack_vectors([jnp.sum(dqkv[0], axis=0, dtype=F32)]),
            pack_vectors([jnp.sum(dqkv[2], axis=0, dtype=F32), dhidden_bias[0]]),
        ],
        axis=2,
    )

    dattn_got, dfirst_after, outputs, dfirst_own, proj_grad, early = join(
        dattn_got, dfirst_after, outputs, dfirst_own, proj_grad, early
    )
    dattn_keep = add_low(dattn_w[0], dattn_got[1])
    dattn_keep, dattn_got = scatter_raw(*split_add(dattn_keep, dattn_got[0]), near[::-1])
    _, pull_one = jax.vjp(layer_norm, residual, gain_one[0], shift_one[0])
    dresidual, gain_own, shift_own = pull_one(dfirst_own + dfirst_after.astype(F32))
    late = pick(pack_vectors([gain_own, shift_own]), inverse(blocks))
    vectors = jnp.concatenate([late, early], axis=2)
    vectors = scatter_pack(vectors, bits)
    order = [0, 1, 4, 5, 6, 8, 2, 3, 7]
    parts = unpack_vectors(vectors, [shards[i] for i in order])
    vector_grads = [parts[order.index(i)] for i in range(len(order))]

    dinputs = reorder(dmiddle + dresidual, blocks, back=True)

    dattn_got, vector_grads, dinputs, dfc_parts = join(
        dattn_got, vector_grads, dinputs, dfc_parts
    )
    fc_grad = total_tp(dfc_parts)[0]
    attn_parts = scatter_tp_raw(add_low(dattn_keep, dattn_got))
    attn_grad = total_tp(attn_parts)
    return (
        outputs,
        dinputs,
        attn_grad[:3],
        attn_grad[3].T,
        fc_grad,
        proj_grad,
        *vector_grads,
    )


def solution(mesh):
    vector = P(("fsdp", "tp"))
    tokens = P(("fsdp", "tp"), None)
    weights = (P(None, "fsdp", "tp"), P("tp", "fsdp"), P("fsdp", "tp"), P("tp", "fsdp"))
    return jax.shard_map(
        per_device,
        mesh=mesh,
        in_specs=(tokens, P("fsdp", None), *weights, *([vector] * 9), tokens),
        out_specs=(tokens, tokens, *weights, *([vector] * 9)),
        check_vma=False,
    )
```
